512 devices in a mesh: clus: 32 (over z, core), grp: 16 (over x, y).
Axes of the slice: x: 4, y: 4, z: 16, core: 2. Of those that a mesh axis runs over, the one named last changes fastest.
Arguments:
- features: bfloat16 [32, 16, 1024, 256], P('clus', 'grp'), may hold values from -6 to 6
- history: bfloat16 [32, 16, 1024, 256], P('clus', 'grp'), may hold values from -6 to 6
- aux_history: bfloat16 [32, 16, 1024, 256], P('clus', 'grp'), may hold values from -0.625 to 0.625
- tile_values: bfloat16 [32, 16, 8, 4, 128, 128], P('clus', 'grp'), may hold values from -0.25 to 0.25
- tile_sources: int32 [32, 16, 8, 4], P('clus', 'grp'), may hold values from 0 to 39, as said below
- send_list: int32 [32, 16, 16, 2], P('clus', 'grp'), may hold values from 0 to 8, as said below
- event_bins: int32 [32, 16, 1024], P('clus', 'grp'), may hold values from 0 to 31
- event_flags: int32 [32, 16, 1024], P('clus', 'grp'), may hold values 0 or 1
- neigh_first: bfloat16 [256, 256], replicated, may hold values from -0.375 to 0.375
- self_first: bfloat16 [256, 256], replicated, may hold values from -0.375 to 0.375
- neigh_second: bfloat16 [256, 256], replicated, may hold values from -0.375 to 0.375
- self_second: bfloat16 [256, 256], replicated, may hold values from -0.375 to 0.375
- hazard_weight: bfloat16 [256, 32], replicated, may hold values from -0.375 to 0.375
Outputs:
- new_history: bfloat16 [32, 16, 1024, 256], P('clus', 'grp')
- grad_hidden: bfloat16 [32, 16, 1024, 256], P('clus', 'grp')
- new_aux: bfloat16 [32, 16, 1024, 256], P('clus', 'grp')
- grad_neigh_first: float32 [256, 256], replicated
- grad_self_first: float32 [256, 256], replicated
- grad_neigh_second: float32 [256, 256], replicated
- grad_self_second: float32 [256, 256], replicated
- grad_hazard: float32 [256, 32], replicated
- loss: float32 [], replicated
The draws below stay inside these ranges and needn't reach their ends.
Inputs may be any that keep to these rules, and one draw needn't show every extreme that they name: `send_list`: entry [c, g, p, s] names the block of device (c, g) sent to device (c, p) in slot s, or 8 for an empty slot; live slots come first in a list; a device's list to itself is empty; every other list has one or two live slots, and every device has at least one full list and at least one list with a single live slot. `tile_sources`: indexes the device's source table; never an empty slot; every live received slot is read by some tile.
All inputs are finite; a program needn't handle non-finite values. No bound on the sum of `event_flags` on one device may be relied on, other than what follows from the above.
Results may differ from the reference program's by a relative error of at most 0.014.
Values may be sent and summed in bfloat16 or wider, within the bound.
A program may use at most 64 MiB of HBM per device.

```python
import jax
import jax.numpy as jnp
from jax import lax

D = 256
TB = 32
BLK = 128
NB = 8
K = 4
S = 2
ROWS = 1024
N_CLUS = 32
N_GRP = 16


def routing_tables(key):
    routing_key = jax.random.fold_in(key, 7)
    key_count, key_block, key_pick, key_order = jax.random.split(routing_key, 4)
    device_col = jnp.arange(N_GRP, dtype=jnp.int32)[:, None]
    peer_row = jnp.arange(N_GRP, dtype=jnp.int32)[None, :]
    counts = jax.random.randint(key_count, (N_CLUS, N_GRP, N_GRP), 1, S + 1)
    counts = jnp.where(peer_row == (device_col + 2) % N_GRP, 1, counts)
    counts = jnp.where(peer_row == (device_col + 1) % N_GRP, S, counts)
    counts = jnp.where(peer_row == device_col, 0, counts)
    blocks = jax.random.randint(key_block, (N_CLUS, N_GRP, N_GRP, S), 0, NB)
    slot_index = jnp.arange(S, dtype=jnp.int32)
    routing = jnp.where(slot_index < counts[..., None], blocks, NB).astype(jnp.int32)
    live_slot = (jnp.swapaxes(routing, 1, 2) < NB).reshape(N_CLUS, N_GRP, N_GRP * S)
    tile_total = NB * K
    drawn = jax.random.randint(key_pick, (N_CLUS, N_GRP, tile_total), 0, NB + N_GRP * S)
    remote = jnp.clip(drawn - NB, 0, N_GRP * S - 1)
    drawn_live = (drawn >= NB) & jnp.take_along_axis(live_slot, remote, axis=2)
    fallback = jnp.where(drawn_live, drawn, drawn % NB)
    position = jnp.arange(tile_total, dtype=jnp.int32)
    cover_slot = jnp.broadcast_to(jnp.clip(position, 0, N_GRP * S - 1), (N_CLUS, N_GRP, tile_total))
    covering = (position < N_GRP * S) & jnp.take_along_axis(live_slot, cover_slot, axis=2)
    chosen = jnp.where(covering, NB + position, fallback)
    scores = jax.random.randint(key_order, (N_CLUS, N_GRP, tile_total), 0, 1 << 20) * tile_total + position
    ordering = jnp.argsort(scores, axis=2)
    chosen = jnp.take_along_axis(chosen, ordering, axis=2)
    return (routing, chosen.reshape(N_CLUS, N_GRP, NB, K).astype(jnp.int32))


def draw_send_list(key, part):
    return routing_tables(key)[0]


def draw_tile_sources(key, part):
    return routing_tables(key)[1]


def plant(values, key, least, top_value):
    longest = values.shape.index(max(values.shape))
    spots = []
    for shift in (0, 1):
        where = [jax.random.randint(jax.random.fold_in(key, axis), (), 0, length) for axis, length in enumerate(values.shape)]
        where[longest] = (where[longest] + shift) % values.shape[longest]
        spots.append(tuple(where))
    return values.at[spots[0]].set(least).at[spots[1]].set(top_value)


def levels(stream_key, extent, pieces, low, high):
    level, own = 1.0, jax.random.fold_in(stream_key, 6)
    for dim, parts in pieces:
        steps = jnp.exp(jax.random.uniform(jax.random.fold_in(own, dim), (parts,), jnp.float32, low / len(pieces), high / len(pieces)))
        level = level * jnp.repeat(steps, extent[dim] // parts).reshape([-1 if axis == dim else 1 for axis in range(len(extent))])
    return level


def noise(rng, dims, scale, reach, cuts=(), held_as=jnp.bfloat16):
    values = scale * jax.random.normal(rng, dims, jnp.float32)
    if cuts:
        values = values * levels(rng, dims, cuts, -0.22, 0.18)
    return jnp.clip(values, -reach, reach).astype(held_as)


def setup_inputs(seed: int = 0) -> dict:
    keys = jax.random.split(jax.random.key(seed), 14)
    return {
        "features": noise(keys[0], (N_CLUS, N_GRP, ROWS, D), 1.0, 6.0, ((0, 32), (1, 16))),
        "history": noise(keys[1], (N_CLUS, N_GRP, ROWS, D), 1.0, 6.0, ((0, 32), (1, 16))),
        "aux_history": noise(keys[2], (N_CLUS, N_GRP, ROWS, D), 0.1, 0.625, ((0, 32), (1, 16))),
        "tile_values": noise(keys[3], (N_CLUS, N_GRP, NB, K, BLK, BLK), (K * BLK) ** -0.5, 0.25, ((0, 32), (1, 16))),
        "tile_sources": draw_tile_sources(jax.random.fold_in(keys[13], 71), 0),
        "send_list": draw_send_list(jax.random.fold_in(keys[13], 71), 0),
        "event_bins": plant(jax.random.randint(keys[6], (N_CLUS, N_GRP, ROWS), 0, TB), jax.random.fold_in(keys[6], 1), 0, TB - 1).astype(jnp.int32),
        "event_flags": plant((jax.random.randint(keys[7], (N_CLUS, N_GRP, ROWS), 0, 10) < 7).astype(jnp.int32), jax.random.fold_in(keys[7], 1), 0, 1),
        "neigh_first": noise(keys[8], (D, D), D ** -0.5, 0.375),
        "self_first": noise(keys[9], (D, D), D ** -0.5, 0.375),
        "neigh_second": noise(keys[10], (D, D), D ** -0.5, 0.375),
        "self_second": noise(keys[11], (D, D), D ** -0.5, 0.375),
        "hazard_weight": noise(keys[12], (D, TB), D ** -0.5, 0.375),
    }


def silu_slope(preact):
    logistic = jax.nn.sigmoid(preact)
    return logistic * (1.0 + preact * (1.0 - logistic))


def aggregate(source_table, sources, tile_vals):
    picked = source_table[sources]
    return jnp.einsum("bkij,bkjd->bid", tile_vals.astype(jnp.float32), picked.astype(jnp.float32))


def spread_back(tile_vals, sources, grad_blocks, table_size):
    contribution = jnp.einsum("bkij,bid->bkjd", tile_vals.astype(jnp.float32), grad_blocks.astype(jnp.float32))
    flattened = contribution.reshape((-1,) + contribution.shape[2:])
    return jax.ops.segment_sum(flattened, sources.reshape(-1), num_segments=table_size)


def transpose_dot(former, latter):
    return jnp.dot(former.T, latter, preferred_element_type=jnp.float32)


def reference(features, history, aux_history, tile_values, tile_sources, send_list, event_bins, event_flags, neigh_first, self_first, neigh_second, self_second, hazard_weight):
    def one_batch(packed):
        feat, past, aux_rows, tile_vals, sources, routing, event_bin, event_flag = packed
        group_size, node_rows, feat_width = feat.shape
        block_count = tile_vals.shape[1]
        block_rows = tile_vals.shape[3]
        slot_count = routing.shape[2]
        row_scale = 1.0 / (group_size * node_rows)
        flat_rows = group_size * node_rows

        def received(values):
            blocks = values.reshape(group_size, block_count, block_rows, feat_width)
            clamped = jnp.minimum(routing, block_count - 1)
            outbound = jax.vmap(lambda block_set, index_set: block_set[index_set])(blocks, clamped)
            outbound = jnp.where((routing < block_count)[..., None, None], outbound, jnp.zeros((), values.dtype))
            return jnp.swapaxes(outbound, 0, 1)

        def table_of(values, incoming):
            own = values.reshape(group_size, block_count, block_rows, feat_width)
            return jnp.concatenate([own, incoming.reshape(group_size, group_size * slot_count, block_rows, feat_width)], axis=1)

        agg_first = jax.vmap(aggregate)(table_of(feat, received(feat)), sources, tile_vals).astype(jnp.bfloat16).reshape(flat_rows, feat_width)
        feat_flat = feat.reshape(flat_rows, feat_width)
        pre_first = jnp.dot(agg_first, neigh_first, preferred_element_type=jnp.float32) + jnp.dot(feat_flat, self_first, preferred_element_type=jnp.float32)
        hidden_first = jax.nn.silu(pre_first).astype(jnp.bfloat16)
        agg_second = jax.vmap(aggregate)(table_of(hidden_first, received(past)), sources, tile_vals).astype(jnp.bfloat16).reshape(flat_rows, feat_width)
        pre_second = jnp.dot(agg_second, neigh_second, preferred_element_type=jnp.float32) + jnp.dot(hidden_first, self_second, preferred_element_type=jnp.float32)
        hidden_second = jax.nn.silu(pre_second).astype(jnp.bfloat16)
        logits = jnp.dot(hidden_second, hazard_weight, preferred_element_type=jnp.float32)
        bins_col = event_bin.reshape(flat_rows, 1)
        flag_col = event_flag.reshape(flat_rows, 1).astype(jnp.float32)
        step_row = jnp.arange(logits.shape[1], dtype=jnp.int32)[None, :]
        counted = step_row <= bins_col
        at_event = (step_row == bins_col).astype(jnp.float32)
        node_loss = jnp.sum(jnp.where(counted, jax.nn.softplus(logits), 0.0), axis=1) - flag_col[:, 0] * jnp.sum(at_event * logits, axis=1)
        batch_loss = jnp.sum(node_loss) * row_scale
        grad_logits = (jnp.where(counted, jax.nn.sigmoid(logits), 0.0) - flag_col * at_event).astype(jnp.bfloat16)
        grad_hazard = transpose_dot(hidden_second, grad_logits) * row_scale
        grad_pre_second = (jnp.dot(grad_logits, hazard_weight.T, preferred_element_type=jnp.float32) * silu_slope(pre_second)).astype(jnp.bfloat16)
        grad_neigh_second = transpose_dot(agg_second, grad_pre_second) * row_scale
        grad_self_second = transpose_dot(hidden_first, grad_pre_second) * row_scale
        grad_agg = jnp.dot(grad_pre_second, neigh_second.T, preferred_element_type=jnp.float32).astype(jnp.bfloat16)
        table_size = block_count + group_size * slot_count
        grad_table = jax.vmap(lambda tv, sr, gb: spread_back(tv, sr, gb, table_size))(tile_vals, sources, grad_agg.reshape(group_size, block_count, block_rows, feat_width))
        sent_back = grad_table[:, block_count:].astype(jnp.bfloat16).reshape(group_size, group_size, slot_count, block_rows, feat_width)
        came_back = jnp.swapaxes(sent_back, 0, 1).astype(jnp.float32)
        selector = (routing[..., None] == jnp.arange(block_count, dtype=jnp.int32)).astype(jnp.float32)
        new_aux = jnp.einsum("gpsj,gpsid->gjid", selector, came_back).astype(jnp.bfloat16).reshape(flat_rows, feat_width)
        grad_total = grad_table[:, :block_count].reshape(flat_rows, feat_width) + jnp.dot(grad_pre_second, self_second.T, preferred_element_type=jnp.float32) + aux_rows.reshape(flat_rows, feat_width).astype(jnp.float32)
        grad_hidden = grad_total.astype(jnp.bfloat16)
        grad_pre_first = (grad_total * silu_slope(pre_first)).astype(jnp.bfloat16)
        grad_neigh_first = transpose_dot(agg_first, grad_pre_first) * row_scale
        grad_self_first = transpose_dot(feat_flat, grad_pre_first) * row_scale
        shape_back = (group_size, node_rows, feat_width)
        return (hidden_first.reshape(shape_back), grad_hidden.reshape(shape_back), new_aux.reshape(shape_back), grad_neigh_first, grad_self_first, grad_neigh_second, grad_self_second, grad_hazard, batch_loss)

    results = lax.map(one_batch, (features, history, aux_history, tile_values, tile_sources, send_list, event_bins, event_flags))
    return (results[0], results[1], results[2], jnp.sum(results[3], axis=0), jnp.sum(results[4], axis=0), jnp.sum(results[5], axis=0), jnp.sum(results[6], axis=0), jnp.sum(results[7], axis=0), jnp.sum(results[8]))
```

```python
import functools

import jax
import jax.numpy as jnp
from jax import lax
from jax.experimental import pallas as pl
from jax.experimental.pallas import tpu as pltpu
from jax.sharding import PartitionSpec as P

MESH = pl.DeviceIdType.MESH
PIECE = 40
UNITS = 10


def owner(unit, depth):
    return (unit * depth) // UNITS


def reduce_kernel(groups, depth, x_ref, o_ref, acc, from_core, from_grp, mine, from_z, done,
                  core_sem, grp_send, grp_recv, z_send, z_recv, zb_send, zb_recv,
                  back_send, back_recv, fwd_send, fwd_recv):
    clus = lax.axis_index("clus")
    g = lax.axis_index("grp")
    core = lax.rem(clus, 2)
    z = clus // 2
    sibling = clus + 1 - 2 * core

    def grp_peer(d):
        return lax.rem(g + d, groups)

    def z_peer(d):
        return lax.rem(z + d, depth)

    barrier = pltpu.get_barrier_semaphore()
    pl.semaphore_signal(barrier, inc=1, device_id={"clus": sibling}, device_id_type=MESH)

    @pl.loop(1, groups)
    def _(d):
        pl.semaphore_signal(barrier, inc=1, device_id={"grp": grp_peer(d)}, device_id_type=MESH)

    @pl.loop(1, depth)
    def _(d):
        pl.semaphore_signal(
            barrier, inc=1, device_id={"clus": z_peer(d) * 2 + core}, device_id_type=MESH
        )

    pl.semaphore_wait(barrier, groups + depth - 1)

    swap = pltpu.make_async_remote_copy(
        src_ref=x_ref.at[1 - core], dst_ref=from_core, send_sem=core_sem.at[0],
        recv_sem=core_sem.at[1], device_id={"clus": sibling}, device_id_type=MESH,
    )
    swap.start()
    swap.wait()
    acc[...] = x_ref[core] + from_core[...]

    def spread(d):
        p = grp_peer(d)
        return pltpu.make_async_remote_copy(
            src_ref=acc.at[p], dst_ref=from_grp.at[g], send_sem=grp_send.at[p],
            recv_sem=grp_recv.at[g], device_id={"grp": p}, device_id_type=MESH,
        )

    def arrived(d):
        p = grp_peer(d)
        return pltpu.make_async_remote_copy(
            src_ref=acc.at[p], dst_ref=from_grp.at[p], send_sem=grp_send.at[p],
            recv_sem=grp_recv.at[p], device_id={"grp": p}, device_id_type=MESH,
        )

    @pl.loop(1, groups)
    def _(d):
        spread(d).start()

    mine[...] = acc[g]

    @pl.loop(1, groups)
    def _(d):
        arrived(d).wait_recv()
        mine[...] += from_grp[grp_peer(d)]

    @pl.loop(1, groups)
    def _(d):
        spread(d).wait_send()

    def unit_of(ref, u):
        return ref.at[pl.ds(8 * (u // 2), 8), pl.ds(128 * (u % 2), 128)]

    def to_owner(u):
        return pltpu.make_async_remote_copy(
            src_ref=unit_of(mine, u), dst_ref=from_z.at[z], send_sem=z_send.at[u],
            recv_sem=z_recv.at[z], device_id={"clus": owner(u, depth) * 2 + core},
            device_id_type=MESH,
        )

    for u in range(UNITS):
        @pl.when(z != owner(u, depth))
        def _():
            to_owner(u).start()

    def share(u, d):
        q = z_peer(d)
        return pltpu.make_async_remote_copy(
            src_ref=unit_of(done, u), dst_ref=unit_of(done, u), send_sem=zb_send.at[q],
            recv_sem=zb_recv.at[u], device_id={"clus": q * 2 + core}, device_id_type=MESH,
        )

    for u in range(UNITS):
        @pl.when(z == owner(u, depth))
        def _():
            def gather(d, total):
                q = z_peer(d)
                pltpu.make_async_remote_copy(
                    src_ref=unit_of(mine, u), dst_ref=from_z.at[q], send_sem=z_send.at[u],
                    recv_sem=z_recv.at[q], device_id={"clus": q * 2 + core}, device_id_type=MESH,
                ).wait_recv()
                return total + from_z[q]

            unit_of(done, u)[...] = lax.fori_loop(1, depth, gather, unit_of(mine, u)[...])

            @pl.loop(1, depth)
            def _(d):
                share(u, d).start()

    for u in range(UNITS):
        @pl.when(z != owner(u, depth))
        def _():
            to_owner(u).wait_send()
            share(u, 1).wait_recv()

    def publish(d):
        p = grp_peer(d)
        return pltpu.make_async_remote_copy(
            src_ref=done, dst_ref=o_ref.at[core, g], send_sem=back_send.at[p],
            recv_sem=back_recv.at[g], device_id={"grp": p}, device_id_type=MESH,
        )

    def forward(half, p):
        return pltpu.make_async_remote_copy(
            src_ref=o_ref.at[half, p], dst_ref=o_ref.at[half, p], send_sem=fwd_send.at[p],
            recv_sem=fwd_recv.at[p], device_id={"clus": sibling}, device_id_type=MESH,
        )

    @pl.loop(1, groups)
    def _(d):
        publish(d).start()

    o_ref[core, g] = done[...]
    forward(core, g).start()

    @pl.loop(1, groups)
    def _(d):
        p = grp_peer(d)
        pltpu.make_async_remote_copy(
            src_ref=done, dst_ref=o_ref.at[core, p], send_sem=back_send.at[p],
            recv_sem=back_recv.at[p], device_id={"grp": p}, device_id_type=MESH,
        ).wait_recv()
        forward(core, p).start()

    @pl.loop(0, groups)
    def _(p):
        forward(core, p).wait_send()
        forward(1 - core, p).wait_recv()

    @pl.loop(1, groups)
    def _(d):
        publish(d).wait_send()

    for u in range(UNITS):
        @pl.when(z == owner(u, depth))
        def _():
            @pl.loop(1, depth)
            def _(d):
                share(u, d).wait_send()


def reduce_all(packed):
    groups = packed.shape[1]
    depth = lax.axis_size("clus") // 2
    width = packed.shape[3]
    dma = pltpu.SemaphoreType.DMA
    return pl.pallas_call(
        functools.partial(reduce_kernel, groups, depth),
        out_shape=jax.ShapeDtypeStruct(packed.shape, jnp.float32),
        in_specs=[pl.BlockSpec(memory_space=pltpu.VMEM)],
        out_specs=pl.BlockSpec(memory_space=pltpu.VMEM),
        scratch_shapes=[
            pltpu.VMEM((groups, PIECE, width), jnp.float32),
            pltpu.VMEM((groups, PIECE, width), jnp.float32),
            pltpu.VMEM((groups, PIECE, width), jnp.float32),
            pltpu.VMEM((PIECE, width), jnp.float32),
            pltpu.VMEM((depth, 8, 128), jnp.float32),
            pltpu.VMEM((PIECE, width), jnp.float32),
            dma((2,)), dma((groups,)), dma((groups,)), dma((UNITS,)), dma((depth,)),
            dma((depth,)), dma((UNITS,)), dma((groups,)), dma((groups,)), dma((groups,)),
            dma((groups,)),
        ],
        compiler_params=pltpu.CompilerParams(
            collective_id=0, has_side_effects=True, vmem_limit_bytes=32 << 20
        ),
    )(packed)


def silu_slope(preact):
    logistic = jax.nn.sigmoid(preact)
    return logistic * (1.0 + preact * (1.0 - logistic))


def aggregate(source_table, sources, tile_vals):
    picked = source_table[sources]
    return jnp.einsum("bkij,bkjd->bid", tile_vals, picked, preferred_element_type=jnp.float32)


def spread_back(tile_vals, sources, grad_blocks, table_size):
    contribution = jnp.einsum(
        "bkij,bid->bkjd", tile_vals, grad_blocks, preferred_element_type=jnp.float32
    )
    flattened = contribution.reshape((-1,) + contribution.shape[2:])
    return jax.ops.segment_sum(flattened, sources.reshape(-1), num_segments=table_size)


def transpose_dot(former, latter):
    return lax.dot_general(
        former, latter, (((0,), (0,)), ((), ())), preferred_element_type=jnp.float32
    )


def dot_by_transpose(former, latter):
    return lax.dot_general(
        former, latter, (((1,), (1,)), ((), ())), preferred_element_type=jnp.float32
    )


def shards(
    features,
    history,
    aux_history,
    tile_values,
    tile_sources,
    send_list,
    event_bins,
    event_flags,
    neigh_first,
    self_first,
    neigh_second,
    self_second,
    hazard_weight,
):
    tile_vals = tile_values[0, 0]
    sources = tile_sources[0, 0]
    routing = send_list[0, 0]
    block_count = tile_vals.shape[0]
    block_rows = tile_vals.shape[2]
    feat_width = features.shape[3]
    peer_count = lax.axis_size("grp")
    slot_count = routing.shape[1]
    node_rows = block_count * block_rows
    row_scale = 1.0 / (node_rows * peer_count)
    table_size = block_count + peer_count * slot_count
    own_rows = features[0, 0]
    past_rows = history[0, 0]
    selector = (
        routing.reshape(-1)[:, None] == jnp.arange(block_count, dtype=jnp.int32)[None, :]
    ).astype(jnp.bfloat16)

    def outgoing(values):
        flattened = values.reshape(block_count, block_rows * feat_width)
        packed = jnp.dot(selector, flattened, preferred_element_type=jnp.float32)
        return packed.astype(jnp.bfloat16).reshape(peer_count, slot_count, block_rows, feat_width)

    def table_of(values, incoming):
        own = values.reshape(block_count, block_rows, feat_width)
        return jnp.concatenate(
            [own, incoming.reshape(peer_count * slot_count, block_rows, feat_width)], axis=0
        )

    feat_in = lax.all_to_all(outgoing(own_rows), "grp", split_axis=0, concat_axis=0, tiled=True)
    agg_first = (
        aggregate(table_of(own_rows, feat_in), sources, tile_vals)
        .astype(jnp.bfloat16)
        .reshape(node_rows, feat_width)
    )
    pre_first = jnp.dot(agg_first, neigh_first, preferred_element_type=jnp.float32) + jnp.dot(
        own_rows, self_first, preferred_element_type=jnp.float32
    )
    hidden_first = jax.nn.silu(pre_first).astype(jnp.bfloat16)
    past_in = lax.all_to_all(outgoing(past_rows), "grp", split_axis=0, concat_axis=0, tiled=True)
    agg_second = (
        aggregate(table_of(hidden_first, past_in), sources, tile_vals)
        .astype(jnp.bfloat16)
        .reshape(node_rows, feat_width)
    )
    pre_second = jnp.dot(agg_second, neigh_second, preferred_element_type=jnp.float32) + jnp.dot(
        hidden_first, self_second, preferred_element_type=jnp.float32
    )
    hidden_second = jax.nn.silu(pre_second).astype(jnp.bfloat16)
    logits = jnp.dot(hidden_second, hazard_weight, preferred_element_type=jnp.float32)
    bins_col = event_bins[0, 0][:, None]
    flag_col = event_flags[0, 0][:, None].astype(jnp.float32)
    step_row = jnp.arange(logits.shape[1], dtype=jnp.int32)[None, :]
    counted = step_row <= bins_col
    at_event = (step_row == bins_col).astype(jnp.float32)
    node_loss = jnp.sum(jnp.where(counted, jax.nn.softplus(logits), 0.0), axis=1) - flag_col[
        :, 0
    ] * jnp.sum(at_event * logits, axis=1)
    part_loss = jnp.sum(node_loss) * row_scale
    grad_logits = (jnp.where(counted, jax.nn.sigmoid(logits), 0.0) - flag_col * at_event).astype(
        jnp.bfloat16
    )
    grad_hazard = transpose_dot(hidden_second, grad_logits) * row_scale
    grad_pre_second = (
        dot_by_transpose(grad_logits, hazard_weight) * silu_slope(pre_second)
    ).astype(jnp.bfloat16)
    grad_neigh_second = transpose_dot(agg_second, grad_pre_second) * row_scale
    grad_self_second = transpose_dot(hidden_first, grad_pre_second) * row_scale
    grad_agg = dot_by_transpose(grad_pre_second, neigh_second).astype(jnp.bfloat16)
    grad_table = spread_back(
        tile_vals, sources, grad_agg.reshape(block_count, block_rows, feat_width), table_size
    )
    sent_back = (
        grad_table[block_count:]
        .astype(jnp.bfloat16)
        .reshape(peer_count, slot_count, block_rows, feat_width)
    )
    came_back = lax.all_to_all(sent_back, "grp", split_axis=0, concat_axis=0, tiled=True)
    aux_sum = transpose_dot(
        selector, came_back.reshape(peer_count * slot_count, block_rows * feat_width)
    )
    new_aux = aux_sum.astype(jnp.bfloat16).reshape(node_rows, feat_width)
    grad_total = (
        grad_table[:block_count].reshape(node_rows, feat_width)
        + dot_by_transpose(grad_pre_second, self_second)
        + aux_history[0, 0].astype(jnp.float32)
    )
    grad_hidden = grad_total.astype(jnp.bfloat16)
    grad_pre_first = (grad_total * silu_slope(pre_first)).astype(jnp.bfloat16)
    grad_neigh_first = transpose_dot(agg_first, grad_pre_first) * row_scale
    grad_self_first = transpose_dot(own_rows, grad_pre_first) * row_scale
    halves = lambda first, second: jnp.stack([first, second]).reshape(2, 16, 16, feat_width)
    loss_row = jnp.broadcast_to(part_loss, (2, 16, 1, feat_width))
    packed = jnp.concatenate(
        [
            halves(grad_neigh_first, grad_self_first),
            halves(grad_neigh_second, grad_self_second),
            grad_hazard.reshape(2, 16, 1, feat_width),
            loss_row,
            jnp.zeros((2, 16, 6, feat_width), jnp.float32),
        ],
        axis=2,
    )
    summed = reduce_all(packed)
    grad_neigh_first, grad_self_first = summed[:, :, 0:16].reshape(2, feat_width, feat_width)
    grad_neigh_second, grad_self_second = summed[:, :, 16:32].reshape(2, feat_width, feat_width)
    grad_hazard = summed[:, :, 32].reshape(grad_hazard.shape)
    part_loss = summed[0, 0, 33, 0]
    return (
        hidden_first[None, None],
        grad_hidden[None, None],
        new_aux[None, None],
        grad_neigh_first,
        grad_self_first,
        grad_neigh_second,
        grad_self_second,
        grad_hazard,
        part_loss,
    )


def solution(mesh):
    in_specs = (
        P("clus", "grp", None, None),
        P("clus", "grp", None, None),
        P("clus", "grp", None, None),
        P("clus", "grp", None, None, None, None),
        P("clus", "grp", None, None),
        P("clus", "grp", None, None),
        P("clus", "grp", None),
        P("clus", "grp", None),
        P(),
        P(),
        P(),
        P(),
        P(),
    )
    out_specs = (
        P("clus", "grp", None, None),
        P("clus", "grp", None, None),
        P("clus", "grp", None, None),
        P(),
        P(),
        P(),
        P(),
        P(),
        P(),
    )
    return jax.shard_map(shards, mesh=mesh, in_specs=in_specs, out_specs=out_specs, check_vma=False)
```

```python
import functools

import jax
import jax.numpy as jnp
from jax import lax
from jax.experimental import pallas as pl
from jax.experimental.pallas import tpu as pltpu
from jax.sharding import PartitionSpec as P

MESH = pl.DeviceIdType.MESH
F32 = jnp.float32
BF16 = jnp.bfloat16
NB = 8
K = 4
S = 2
BLK = 128
D = 256
TB = 32
TILES = NB * K
CHUNK = 2
ROWS = CHUNK * BLK
CHUNKS = NB // CHUNK
LANES = 128


def nn(a, b):
    return jnp.dot(a, b, preferred_element_type=F32)


def nt(a, b):
    return lax.dot_general(a, b, (((1,), (1,)), ((), ())), preferred_element_type=F32)


def tn(a, b):
    return lax.dot_general(a, b, (((0,), (0,)), ((), ())), preferred_element_type=F32)


def sigmoid(v):
    return 0.5 * jnp.tanh(0.5 * v) + 0.5


def slope(v):
    q = sigmoid(v)
    return q * (1.0 + v * (1.0 - q))


def program_kernel(
    groups, depth,
    tab, feat_in, hist_in, aux_in, tiles_in, bins, flags, w_nf, w_sf, w_ns, w_ss, w_hz,
    o_hist, o_hidden, o_aux, o_nf, o_sf, o_ns, o_ss, o_hz, o_loss,
    own, past, aux, tiles, turned, table1, table2, stage1, stage2, agg1, agg2, pre1, hid2, gp2,
    gp1, glog, chain, came, fold, loss_acc,
    pack, total, acc, from_core, from_grp, mine, from_z, done,
    load_sem, f_send, f_recv, h_send, h_recv, b_send, b_recv,
    core_sem, g_send, g_recv, z_send, z_recv, zb_send, zb_recv, r_send, r_recv, w_send, w_recv,
):
    slots = groups * S
    t_src = 0
    t_snd = t_src + TILES
    t_prev = t_snd + slots
    t_last = t_prev + TILES
    t_qprev = t_last + NB + slots
    t_qlast = t_qprev + slots
    rows_of = D // groups
    piece = 2 * rows_of + 8
    units = piece // 4
    scale = 1.0 / (NB * BLK * groups)

    clus = lax.axis_index("clus")
    g = lax.axis_index("grp")
    core = lax.rem(clus, 2)
    z = clus // 2
    sibling = clus + 1 - 2 * core

    def grp_peer(d):
        return lax.rem(g + d, groups)

    def z_peer(d):
        return lax.rem(z + d, depth)

    loads = [
        pltpu.make_async_copy(feat_in, own, load_sem.at[0]),
        pltpu.make_async_copy(hist_in, past, load_sem.at[1]),
        pltpu.make_async_copy(feat_in, table1.at[pl.ds(0, NB)], load_sem.at[2]),
        pltpu.make_async_copy(tiles_in, tiles, load_sem.at[3]),
        pltpu.make_async_copy(aux_in, aux, load_sem.at[4]),
    ]
    for load in loads:
        load.start()

    barrier = pltpu.get_barrier_semaphore()
    pl.semaphore_signal(barrier, inc=1, device_id={"clus": sibling}, device_id_type=MESH)

    @pl.loop(1, groups)
    def _(d):
        pl.semaphore_signal(barrier, inc=1, device_id={"grp": grp_peer(d)}, device_id_type=MESH)

    @pl.loop(1, depth)
    def _(d):
        pl.semaphore_signal(
            barrier, inc=1, device_id={"clus": z_peer(d) * 2 + core}, device_id_type=MESH
        )

    blank = jnp.zeros((S, BLK, D), BF16)
    table1[pl.ds(NB + g * S, S)] = blank
    table2[pl.ds(NB + g * S, S)] = blank
    came[pl.ds(g * S, S)] = blank
    chain[TILES] = jnp.zeros((BLK, D), F32)
    fold[slots] = jnp.zeros((BLK, D), F32)
    pack[:, :, 2 * rows_of :, :] = jnp.zeros((2, groups, 8, D), F32)

    pl.semaphore_wait(barrier, groups + depth - 1)

    def exchange(stage, target, base, send, recv):
        def out(d):
            p = grp_peer(d)
            return pltpu.make_async_remote_copy(
                src_ref=stage.at[pl.ds(p * S, S)], dst_ref=target.at[pl.ds(base + g * S, S)],
                send_sem=send.at[p], recv_sem=recv.at[g],
                device_id={"grp": p}, device_id_type=MESH,
            )

        def into(d):
            p = grp_peer(d)
            return pltpu.make_async_remote_copy(
                src_ref=stage.at[pl.ds(p * S, S)], dst_ref=target.at[pl.ds(base + p * S, S)],
                send_sem=send.at[p], recv_sem=recv.at[p],
                device_id={"grp": p}, device_id_type=MESH,
            )

        return out, into

    f_out, f_in = exchange(stage1, table1, NB, f_send, f_recv)
    h_out, h_in = exchange(stage2, table2, NB, h_send, h_recv)
    b_out, b_in = exchange(stage1, came, 0, b_send, b_recv)

    loads[0].wait()

    @pl.loop(1, groups)
    def _(d):
        p = grp_peer(d)
        for s in range(S):
            stage1[p * S + s] = own[tab[t_snd + p * S + s]]
        f_out(d).start()

    loads[1].wait()

    @pl.loop(1, groups)
    def _(d):
        p = grp_peer(d)
        for s in range(S):
            stage2[p * S + s] = past[tab[t_snd + p * S + s]]
        f_out(d).wait_send()
        h_out(d).start()

    loads[3].wait()

    @pl.loop(0, NB)
    def _(b):
        for k in range(K):
            turned[b, pl.ds(k * BLK, BLK), :] = tiles[b, k].T

    loads[2].wait()

    @pl.loop(1, groups)
    def _(d):
        f_in(d).wait_recv()

    def aggregate(table, b):
        wide = jnp.concatenate([tiles[b, k] for k in range(K)], axis=1)
        deep = jnp.concatenate([table[tab[t_src + b * K + k]] for k in range(K)], axis=0)
        return nn(wide, deep).astype(BF16)

    @pl.loop(0, CHUNKS)
    def _(c):
        a = jnp.concatenate([aggregate(table1, c * CHUNK + j) for j in range(CHUNK)], axis=0)
        rows = pl.ds(pl.multiple_of(c * ROWS, ROWS), ROWS)
        blocks = pl.ds(c * CHUNK, CHUNK)
        agg1[rows, :] = a
        pre = nn(a, w_nf[...]) + nn(own[blocks].reshape(ROWS, D), w_sf[...])
        pre1[rows, :] = pre
        h = (pre * sigmoid(pre)).astype(BF16)
        table2[blocks] = h.reshape(CHUNK, BLK, D)
        o_hist[rows, :] = h

    loss_acc[...] = jnp.zeros((TB, ROWS), F32)

    @pl.loop(1, groups)
    def _(d):
        h_in(d).wait_recv()

    @pl.loop(0, CHUNKS)
    def _(c):
        a = jnp.concatenate([aggregate(table2, c * CHUNK + j) for j in range(CHUNK)], axis=0)
        rows = pl.ds(pl.multiple_of(c * ROWS, ROWS), ROWS)
        blocks = pl.ds(c * CHUNK, CHUNK)
        agg2[rows, :] = a
        pre = nn(a, w_ns[...]) + nn(table2[blocks].reshape(ROWS, D), w_ss[...])
        q = sigmoid(pre)
        h = (pre * q).astype(BF16)
        hid2[rows, :] = h
        logits = nt(w_hz[...], h)
        step = lax.broadcasted_iota(jnp.int32, (TB, ROWS), 0)
        bin_row = bins[c]
        flag_row = flags[c].astype(F32)
        counted = step <= bin_row
        event = jnp.where(step == bin_row, flag_row, 0.0)
        soft = jnp.maximum(logits, 0.0) + jnp.log1p(jnp.exp(-jnp.abs(logits)))
        loss_acc[...] += jnp.where(counted, soft, 0.0) - event * logits
        gl = (jnp.where(counted, sigmoid(logits), 0.0) - event).astype(BF16)
        glog[:, rows] = gl
        gp = (tn(gl, w_hz[...]) * (q * (1.0 + pre * (1.0 - q)))).astype(BF16)
        gp2[rows, :] = gp
        ga = nt(gp, w_ns[...]).astype(BF16)
        for j in range(CHUNK):
            b = c * CHUNK + j
            spread = nn(turned[b], ga[j * BLK : (j + 1) * BLK])
            for k in range(K):
                i = b * K + k
                chain[i] = spread[k * BLK : (k + 1) * BLK] + chain[tab[t_prev + i]]

    @pl.loop(1, groups)
    def _(d):
        p = grp_peer(d)
        for s in range(S):
            stage1[p * S + s] = chain[tab[t_last + NB + p * S + s]].astype(BF16)
        b_out(d).start()

    loads[4].wait()

    def put(half, base, value):
        pack[half, :, pl.ds(base, rows_of), :] = (value * scale).reshape(groups, rows_of, D)

    put(0, rows_of, tn(agg2[...], gp2[...]))
    put(1, rows_of, tn(table2[pl.ds(0, NB)].reshape(NB * BLK, D), gp2[...]))
    hz = nn(glog[...], hid2[...]) * scale
    for t in range(TB // 8):
        pack[t // 2, t % 2, pl.ds(2 * rows_of, 8), :] = hz[t * 8 : (t + 1) * 8]
    loss = jnp.sum(loss_acc[...], keepdims=True) * scale
    pack[0, 2, pl.ds(2 * rows_of, 8), :] = jnp.broadcast_to(loss, (8, D))

    @pl.loop(0, CHUNKS)
    def _(c):
        rows = pl.ds(pl.multiple_of(c * ROWS, ROWS), ROWS)
        local = jnp.concatenate(
            [chain[tab[t_last + c * CHUNK + j]] for j in range(CHUNK)], axis=0
        )
        grad = local + nt(gp2[rows, :], w_ss[...]) + aux[rows, :].astype(F32)
        o_hidden[rows, :] = grad.astype(BF16)
        gp1[rows, :] = (grad * slope(pre1[rows, :])).astype(BF16)

    put(0, 0, tn(agg1[...], gp1[...]))
    put(1, 0, tn(own[...].reshape(NB * BLK, D), gp1[...]))

    swap = pltpu.make_async_remote_copy(
        src_ref=pack.at[1 - core], dst_ref=from_core, send_sem=core_sem.at[0],
        recv_sem=core_sem.at[1], device_id={"clus": sibling}, device_id_type=MESH,
    )
    swap.start()
    swap.wait()
    acc[...] = pack[core] + from_core[...]

    def spread_out(d):
        p = grp_peer(d)
        return pltpu.make_async_remote_copy(
            src_ref=acc.at[p], dst_ref=from_grp.at[g], send_sem=g_send.at[p],
            recv_sem=g_recv.at[g], device_id={"grp": p}, device_id_type=MESH,
        )

    @pl.loop(1, groups)
    def _(d):
        spread_out(d).start()

    mine[...] = acc[g]

    @pl.loop(1, groups)
    def _(d):
        b_in(d).wait_recv()

    @pl.loop(0, slots)
    def _(i):
        fold[i] = came[i].astype(F32) + fold[tab[t_qprev + i]]

    @pl.loop(0, NB)
    def _(j):
        o_aux[j] = fold[tab[t_qlast + j]].astype(BF16)

    @pl.loop(1, groups)
    def _(d):
        p = grp_peer(d)
        pltpu.make_async_remote_copy(
            src_ref=acc.at[p], dst_ref=from_grp.at[p], send_sem=g_send.at[p],
            recv_sem=g_recv.at[p], device_id={"grp": p}, device_id_type=MESH,
        ).wait_recv()
        mine[...] += from_grp[p]

    def owner(u):
        return (u * depth) // units

    def lot(u):
        return u if depth < units else 0

    def unit_of(ref, u):
        return ref.at[pl.ds(8 * (u // 2), 8), pl.ds(LANES * (u % 2), LANES)]

    def to_owner(u):
        return pltpu.make_async_remote_copy(
            src_ref=unit_of(mine, u), dst_ref=from_z.at[lot(u), z], send_sem=z_send.at[u],
            recv_sem=z_recv.at[lot(u), z], device_id={"clus": owner(u) * 2 + core},
            device_id_type=MESH,
        )

    for u in range(units):
        @pl.when(z != owner(u))
        def _():
            to_owner(u).start()

    def share(u, d):
        q = z_peer(d)
        return pltpu.make_async_remote_copy(
            src_ref=unit_of(done, u), dst_ref=unit_of(done, u), send_sem=zb_send.at[lot(u), q],
            recv_sem=zb_recv.at[u], device_id={"clus": q * 2 + core}, device_id_type=MESH,
        )

    for u in range(units):
        @pl.when(z == owner(u))
        def _():
            def gather(d, partial):
                q = z_peer(d)
                pltpu.make_async_remote_copy(
                    src_ref=unit_of(mine, u), dst_ref=from_z.at[lot(u), q],
                    send_sem=z_send.at[u], recv_sem=z_recv.at[lot(u), q],
                    device_id={"clus": q * 2 + core}, device_id_type=MESH,
                ).wait_recv()
                return partial + from_z[lot(u), q]

            unit_of(done, u)[...] = lax.fori_loop(1, depth, gather, unit_of(mine, u)[...])

            @pl.loop(1, depth)
            def _(d):
                share(u, d).start()

    for u in range(units):
        @pl.when(z != owner(u))
        def _():
            to_owner(u).wait_send()
            share(u, 1).wait_recv()

    def publish(d, slot):
        p = grp_peer(d)
        return pltpu.make_async_remote_copy(
            src_ref=done, dst_ref=total.at[core, slot], send_sem=r_send.at[p],
            recv_sem=r_recv.at[slot], device_id={"grp": p}, device_id_type=MESH,
        )

    def forward(half, p):
        return pltpu.make_async_remote_copy(
            src_ref=total.at[half, p], dst_ref=total.at[half, p], send_sem=w_send.at[p],
            recv_sem=w_recv.at[p], device_id={"clus": sibling}, device_id_type=MESH,
        )

    @pl.loop(1, groups)
    def _(d):
        publish(d, g).start()

    total[core, g] = done[...]
    forward(core, g).start()

    @pl.loop(1, groups)
    def _(d):
        p = grp_peer(d)
        publish(d, p).wait_recv()
        forward(core, p).start()

    @pl.loop(0, groups)
    def _(p):
        forward(1 - core, p).wait_recv()

    def pick(half, base):
        return total[half, :, pl.ds(base, rows_of), :].reshape(D, D)

    o_nf[...] = pick(0, 0)
    o_sf[...] = pick(1, 0)
    o_ns[...] = pick(0, rows_of)
    o_ss[...] = pick(1, rows_of)
    for t in range(TB // 8):
        o_hz[pl.ds(t * 8, 8), :] = total[t // 2, t % 2, pl.ds(2 * rows_of, 8), :]
    o_loss[...] = total[0, 2, pl.ds(2 * rows_of, 8), pl.ds(0, LANES)]

    @pl.loop(1, groups)
    def _(d):
        h_out(d).wait_send()
        b_out(d).wait_send()
        spread_out(d).wait_send()
        publish(d, g).wait_send()

    @pl.loop(0, groups)
    def _(p):
        forward(core, p).wait_send()

    for u in range(units):
        @pl.when(z == owner(u))
        def _():
            @pl.loop(1, depth)
            def _(d):
                share(u, d).wait_send()


def latest(keys, queries, limits):
    count = keys.shape[0]
    place = jnp.arange(count, dtype=jnp.int32)[None, :]
    hit = (keys[None, :] == queries[:, None]) & (place < limits[:, None])
    found = jnp.max(jnp.where(hit, place, -1), axis=1)
    return jnp.where(found < 0, count, found)


def shards(
    features, history, aux_history, tile_values, tile_sources, send_list, event_bins, event_flags,
    neigh_first, self_first, neigh_second, self_second, hazard_weight,
):
    groups = lax.axis_size("grp")
    depth = lax.axis_size("clus") // 2
    slots = groups * S
    rows_of = D // groups
    piece = 2 * rows_of + 8
    units = piece // 4
    lots = units if depth < units else 1
    src = tile_sources.reshape(TILES)
    snd = send_list.reshape(slots)
    ints = lambda n: jnp.arange(n, dtype=jnp.int32)
    full = lambda n, v: jnp.full((n,), v, jnp.int32)
    tab = jnp.concatenate(
        [
            src,
            jnp.minimum(snd, NB - 1),
            latest(
                src,
                jnp.concatenate([src, ints(NB + slots)]),
                jnp.concatenate([ints(TILES), full(NB + slots, TILES)]),
            ),
            latest(
                snd,
                jnp.concatenate([snd, ints(NB)]),
                jnp.concatenate([ints(slots), full(NB, slots)]),
            ),
        ]
    )
    any_spec = pl.BlockSpec(memory_space=pl.ANY)
    vmem = pl.BlockSpec(memory_space=pltpu.VMEM)
    dma = pltpu.SemaphoreType.DMA
    nodes = NB * BLK
    out_shape = (
        jax.ShapeDtypeStruct((nodes, D), BF16),
        jax.ShapeDtypeStruct((nodes, D), BF16),
        jax.ShapeDtypeStruct((NB, BLK, D), BF16),
        jax.ShapeDtypeStruct((D, D), F32),
        jax.ShapeDtypeStruct((D, D), F32),
        jax.ShapeDtypeStruct((D, D), F32),
        jax.ShapeDtypeStruct((D, D), F32),
        jax.ShapeDtypeStruct((TB, D), F32),
        jax.ShapeDtypeStruct((8, LANES), F32),
    )
    scratch = [
        pltpu.VMEM((NB, BLK, D), BF16),
        pltpu.VMEM((NB, BLK, D), BF16),
        pltpu.VMEM((nodes, D), BF16),
        pltpu.VMEM((NB, K, BLK, BLK), BF16),
        pltpu.VMEM((NB, K * BLK, BLK), BF16),
        pltpu.VMEM((NB + slots, BLK, D), BF16),
        pltpu.VMEM((NB + slots, BLK, D), BF16),
        pltpu.VMEM((slots, BLK, D), BF16),
        pltpu.VMEM((slots, BLK, D), BF16),
        pltpu.VMEM((nodes, D), BF16),
        pltpu.VMEM((nodes, D), BF16),
        pltpu.VMEM((nodes, D), F32),
        pltpu.VMEM((nodes, D), BF16),
        pltpu.VMEM((nodes, D), BF16),
        pltpu.VMEM((nodes, D), BF16),
        pltpu.VMEM((TB, nodes), BF16),
        pltpu.VMEM((TILES + 1, BLK, D), F32),
        pltpu.VMEM((slots, BLK, D), BF16),
        pltpu.VMEM((slots + 1, BLK, D), F32),
        pltpu.VMEM((TB, ROWS), F32),
        pltpu.VMEM((2, groups, piece, D), F32),
        pltpu.VMEM((2, groups, piece, D), F32),
        pltpu.VMEM((groups, piece, D), F32),
        pltpu.VMEM((groups, piece, D), F32),
        pltpu.VMEM((groups, piece, D), F32),
        pltpu.VMEM((piece, D), F32),
        pltpu.VMEM((lots, depth, 8, LANES), F32),
        pltpu.VMEM((piece, D), F32),
        dma((5,)),
        dma((groups,)), dma((groups,)), dma((groups,)), dma((groups,)), dma((groups,)),
        dma((groups,)),
        dma((2,)), dma((groups,)), dma((groups,)), dma((units,)), dma((lots, depth)),
        dma((lots, depth)), dma((units,)), dma((groups,)), dma((groups,)), dma((groups,)),
        dma((groups,)),
    ]
    outs = pl.pallas_call(
        functools.partial(program_kernel, groups, depth),
        out_shape=out_shape,
        in_specs=[pl.BlockSpec(memory_space=pltpu.SMEM)] + [any_spec] * 4 + [vmem] * 7,
        out_specs=(vmem,) * 9,
        scratch_shapes=scratch,
        compiler_params=pltpu.CompilerParams(
            collective_id=0, has_side_effects=True, vmem_limit_bytes=56 << 20
        ),
    )(
        tab,
        features.reshape(NB, BLK, D),
        history.reshape(NB, BLK, D),
        aux_history.reshape(nodes, D),
        tile_values.reshape(NB, K, BLK, BLK),
        event_bins.reshape(CHUNKS, 1, ROWS),
        event_flags.reshape(CHUNKS, 1, ROWS),
        neigh_first, self_first, neigh_second, self_second, hazard_weight.T,
    )
    hist, hidden, aux, nf, sf, ns, ss, hz, loss = outs
    return (
        hist[None, None], hidden[None, None], aux.reshape(1, 1, nodes, D),
        nf, sf, ns, ss, hz.T, loss[0, 0],
    )


def solution(mesh):
    in_specs = (
        P("clus", "grp", None, None),
        P("clus", "grp", None, None),
        P("clus", "grp", None, None),
        P("clus", "grp", None, None, None, None),
        P("clus", "grp", None, None),
        P("clus", "grp", None, None),
        P("clus", "grp", None),
        P("clus", "grp", None),
        P(), P(), P(), P(), P(),
    )
    out_specs = (
        P("clus", "grp", None, None),
        P("clus", "grp", None, None),
        P("clus", "grp", None, None),
        P(), P(), P(), P(), P(), P(),
    )
    return jax.shard_map(shards, mesh=mesh, in_specs=in_specs, out_specs=out_specs, check_vma=False)
```

```python
import functools

import jax
import jax.numpy as jnp
from jax import lax
from jax.experimental import pallas as pl
from jax.experimental.pallas import tpu as pltpu
from jax.sharding import PartitionSpec as P

MESH = pl.DeviceIdType.MESH
F32 = jnp.float32
BF16 = jnp.bfloat16
NB = 8
K = 4
S = 2
BLK = 128
D = 256
TB = 32
TILES = NB * K
CHUNK = 2
ROWS = CHUNK * BLK
CHUNKS = NB // CHUNK
LANES = 128
PARTS = 4
PART = S * BLK // PARTS
ORDER = (
    (2, 2), (1, 0), (0, 1), (3, 0), (0, 3), (1, 1), (3, 3), (1, 3),
    (3, 1), (2, 0), (0, 2), (2, 1), (1, 2), (2, 3), (3, 2),
)


def nn(a, b):
    return jnp.dot(a, b, preferred_element_type=F32)


def nt(a, b):
    return lax.dot_general(a, b, (((1,), (1,)), ((), ())), preferred_element_type=F32)


def tn(a, b):
    return lax.dot_general(a, b, (((0,), (0,)), ((), ())), preferred_element_type=F32)


def sigmoid(v):
    return 0.5 * jnp.tanh(0.5 * v) + 0.5


def slope(v):
    q = sigmoid(v)
    return q * (1.0 + v * (1.0 - q))


def program_kernel(
    groups, depth,
    tab, feat_in, hist_in, aux_in, tiles_in, bins_in, flags_in, nf_in, sf_in, ns_in, ss_in, hz_in,
    x_hist, x_hidden, x_aux, x_total,
    o_hist, o_hidden, o_aux, bins, flags, w_nf, w_sf, w_ns, w_ss, w_hz,
    own, past, aux, tiles, turned, table1, table2, stage1, stage2, agg1, agg2, pre1, hid2, gp2,
    gp1, glog, chain, came, fold, loss_acc,
    pack, total, acc, narrow, from_core, from_grp, mine, from_z, done, final,
    load_sem, f_send, f_recv, h_send, h_recv, b_send, b_recv,
    core_sem, g_send, g_recv, z_send, z_recv, zb_send, zb_recv, r_send, r_recv, w_send, w_recv,
):
    slots = groups * S
    t_src = 0
    t_snd = t_src + TILES
    t_prev = t_snd + slots
    t_last = t_prev + TILES
    t_qprev = t_last + NB + slots
    t_qlast = t_qprev + slots
    rows_of = D // groups
    piece = 2 * rows_of + 8
    units = piece // 4
    scale = 1.0 / (NB * BLK * groups)

    clus = lax.axis_index("clus")
    g = lax.axis_index("grp")
    core = lax.rem(clus, 2)
    z = clus // 2
    sibling = clus + 1 - 2 * core

    def grp_peer(d):
        return lax.rem(g + d, groups)

    def z_peer(d):
        return lax.rem(z + d, depth)

    side = int(groups ** 0.5)
    gx = g // side
    gy = lax.rem(g, side)
    peers = [
        lax.rem(gx + dx, side) * side + lax.rem(gy + dy, side)
        for dx, dy in ORDER if dx < side and dy < side
    ]

    loads = [
        pltpu.make_async_copy(feat_in, own, load_sem.at[0]),
        pltpu.make_async_copy(hist_in, past, load_sem.at[1]),
        pltpu.make_async_copy(feat_in, table1.at[pl.ds(0, NB)], load_sem.at[2]),
        pltpu.make_async_copy(tiles_in, tiles, load_sem.at[3]),
        pltpu.make_async_copy(aux_in, aux, load_sem.at[4]),
        pltpu.make_async_copy(nf_in, w_nf, load_sem.at[5]),
        pltpu.make_async_copy(sf_in, w_sf, load_sem.at[6]),
        pltpu.make_async_copy(ns_in, w_ns, load_sem.at[7]),
        pltpu.make_async_copy(ss_in, w_ss, load_sem.at[8]),
        pltpu.make_async_copy(hz_in, w_hz, load_sem.at[9]),
        pltpu.make_async_copy(bins_in, bins, load_sem.at[10]),
        pltpu.make_async_copy(flags_in, flags, load_sem.at[11]),
    ]
    for load in loads:
        load.start()

    barrier = pltpu.get_barrier_semaphore()
    pl.semaphore_signal(barrier, inc=1, device_id={"clus": sibling}, device_id_type=MESH)

    @pl.loop(1, groups)
    def _(d):
        pl.semaphore_signal(barrier, inc=1, device_id={"grp": grp_peer(d)}, device_id_type=MESH)

    @pl.loop(1, depth)
    def _(d):
        pl.semaphore_signal(
            barrier, inc=1, device_id={"clus": z_peer(d) * 2 + core}, device_id_type=MESH
        )

    blank = jnp.zeros((S, BLK, D), BF16)
    table1[pl.ds(NB + g * S, S)] = blank
    table2[pl.ds(NB + g * S, S)] = blank
    came[pl.ds(g * S, S)] = blank
    chain[TILES] = jnp.zeros((BLK, D), F32)
    fold[slots] = jnp.zeros((BLK, D), F32)
    pack[:, :, 2 * rows_of :, :] = jnp.zeros((2, groups, 8, D), F32)

    pl.semaphore_wait(barrier, groups + depth - 1)

    def exchange(stage, target, base, send, recv):
        def out(p, part):
            s = part * PART // BLK
            rows = pl.ds(pl.multiple_of(lax.rem(part * PART, BLK), PART), PART)
            return pltpu.make_async_remote_copy(
                src_ref=stage.at[p * S + s, rows], dst_ref=target.at[base + g * S + s, rows],
                send_sem=send.at[p], recv_sem=recv.at[g],
                device_id={"grp": p}, device_id_type=MESH,
            )

        def whole(p):
            return pltpu.make_async_remote_copy(
                src_ref=stage.at[pl.ds(p * S, S)], dst_ref=target.at[pl.ds(base + p * S, S)],
                send_sem=send.at[p], recv_sem=recv.at[p],
                device_id={"grp": p}, device_id_type=MESH,
            )

        def post(load, first, last):
            @pl.loop(first, last)
            def _(part):
                s = part * PART // BLK
                rows = pl.ds(pl.multiple_of(lax.rem(part * PART, BLK), PART), PART)
                for p in peers:
                    stage[p * S + s, rows] = load(p * S + s, rows).astype(BF16)
                    out(p, part).start()

        return post, whole

    f_post, f_whole = exchange(stage1, table1, NB, f_send, f_recv)
    h_post, h_whole = exchange(stage2, table2, NB, h_send, h_recv)
    b_post, b_whole = exchange(stage1, came, 0, b_send, b_recv)

    loads[0].wait()
    f_post(lambda q, rows: own[tab[t_snd + q], rows], 0, PARTS)
    loads[1].wait()
    h_post(lambda q, rows: past[tab[t_snd + q], rows], 0, PARTS)

    loads[3].wait()

    @pl.loop(0, NB)
    def _(b):
        for k in range(K):
            turned[b, pl.ds(k * BLK, BLK), :] = tiles[b, k].T

    for load in loads[4:] + loads[2:3]:
        load.wait()

    @pl.loop(1, groups)
    def _(d):
        f_whole(grp_peer(d)).wait()

    def aggregate(table, b):
        wide = jnp.concatenate([tiles[b, k] for k in range(K)], axis=1)
        deep = jnp.concatenate([table[tab[t_src + b * K + k]] for k in range(K)], axis=0)
        return nn(wide, deep).astype(BF16)

    @pl.loop(0, CHUNKS)
    def _(c):
        a = jnp.concatenate([aggregate(table1, c * CHUNK + j) for j in range(CHUNK)], axis=0)
        rows = pl.ds(pl.multiple_of(c * ROWS, ROWS), ROWS)
        blocks = pl.ds(c * CHUNK, CHUNK)
        agg1[rows, :] = a
        pre = nn(a, w_nf[...]) + nn(own[blocks].reshape(ROWS, D), w_sf[...])
        pre1[rows, :] = pre
        h = (pre * sigmoid(pre)).astype(BF16)
        table2[blocks] = h.reshape(CHUNK, BLK, D)
        o_hist[rows, :] = h

    keeps = [
        pltpu.make_async_copy(o_hist, x_hist, load_sem.at[0]),
        pltpu.make_async_copy(o_hidden, x_hidden, load_sem.at[1]),
        pltpu.make_async_copy(o_aux, x_aux, load_sem.at[2]),
        pltpu.make_async_copy(total, x_total, load_sem.at[3]),
    ]
    keeps[0].start()
    loss_acc[...] = jnp.zeros((TB, ROWS), F32)

    @pl.loop(1, groups)
    def _(d):
        h_whole(grp_peer(d)).wait_recv()

    @pl.loop(0, CHUNKS)
    def _(c):
        a = jnp.concatenate([aggregate(table2, c * CHUNK + j) for j in range(CHUNK)], axis=0)
        rows = pl.ds(pl.multiple_of(c * ROWS, ROWS), ROWS)
        blocks = pl.ds(c * CHUNK, CHUNK)
        agg2[rows, :] = a
        pre = nn(a, w_ns[...]) + nn(table2[blocks].reshape(ROWS, D), w_ss[...])
        q = sigmoid(pre)
        h = (pre * q).astype(BF16)
        hid2[rows, :] = h
        logits = nt(w_hz[...], h)
        step = lax.broadcasted_iota(jnp.int32, (TB, ROWS), 0)
        bin_row = bins[c]
        flag_row = flags[c].astype(F32)
        counted = step <= bin_row
        event = jnp.where(step == bin_row, flag_row, 0.0)
        soft = jnp.maximum(logits, 0.0) + jnp.log1p(jnp.exp(-jnp.abs(logits)))
        loss_acc[...] += jnp.where(counted, soft, 0.0) - event * logits
        gl = (jnp.where(counted, sigmoid(logits), 0.0) - event).astype(BF16)
        glog[:, rows] = gl
        gp = (tn(gl, w_hz[...]) * (q * (1.0 + pre * (1.0 - q)))).astype(BF16)
        gp2[rows, :] = gp
        ga = nt(gp, w_ns[...]).astype(BF16)
        for j in range(CHUNK):
            b = c * CHUNK + j
            spread = nn(turned[b], ga[j * BLK : (j + 1) * BLK])
            for k in range(K):
                i = b * K + k
                chain[i] = spread[k * BLK : (k + 1) * BLK] + chain[tab[t_prev + i]]

    def returned(q, rows):
        return chain[tab[t_last + NB + q], rows]

    b_post(returned, 0, PARTS // 2)

    def put(half, base, value):
        pack[half, :, pl.ds(base, rows_of), :] = (value * scale).reshape(groups, rows_of, D)

    put(0, rows_of, tn(agg2[...], gp2[...]))
    put(1, rows_of, tn(table2[pl.ds(0, NB)].reshape(NB * BLK, D), gp2[...]))
    hz = nn(glog[...], hid2[...]) * scale
    for t in range(TB // 8):
        pack[t // 2, t % 2, pl.ds(2 * rows_of, 8), :] = hz[t * 8 : (t + 1) * 8]
    loss = jnp.sum(loss_acc[...], keepdims=True) * scale
    pack[0, 2, pl.ds(2 * rows_of, 8), :] = jnp.broadcast_to(loss, (8, D))

    @pl.loop(0, CHUNKS)
    def _(c):
        rows = pl.ds(pl.multiple_of(c * ROWS, ROWS), ROWS)
        local = jnp.concatenate(
            [chain[tab[t_last + c * CHUNK + j]] for j in range(CHUNK)], axis=0
        )
        grad = local + nt(gp2[rows, :], w_ss[...]) + aux[rows, :].astype(F32)
        o_hidden[rows, :] = grad.astype(BF16)
        gp1[rows, :] = (grad * slope(pre1[rows, :])).astype(BF16)

    keeps[1].start()
    put(0, 0, tn(agg1[...], gp1[...]))
    put(1, 0, tn(own[...].reshape(NB * BLK, D), gp1[...]))

    swap = pltpu.make_async_remote_copy(
        src_ref=pack.at[1 - core], dst_ref=from_core, send_sem=core_sem.at[0],
        recv_sem=core_sem.at[1], device_id={"clus": sibling}, device_id_type=MESH,
    )
    swap.start()

    swap.wait()
    acc[...] = pack[core] + from_core[...]
    narrow[...] = acc[...].astype(BF16)

    def spread_out(p):
        return pltpu.make_async_remote_copy(
            src_ref=narrow.at[p], dst_ref=from_grp.at[g], send_sem=g_send.at[p],
            recv_sem=g_recv.at[g], device_id={"grp": p}, device_id_type=MESH,
        )

    for p in peers:
        spread_out(p).start()

    b_post(returned, PARTS // 2, PARTS)

    mine[...] = acc[g]

    @pl.loop(1, groups)
    def _(d):
        p = grp_peer(d)
        pltpu.make_async_remote_copy(
            src_ref=narrow.at[p], dst_ref=from_grp.at[p], send_sem=g_send.at[p],
            recv_sem=g_recv.at[p], device_id={"grp": p}, device_id_type=MESH,
        ).wait_recv()
        mine[...] += from_grp[p].astype(F32)

    def owner(u):
        return (u * depth) // units

    def lot(u):
        return u if depth < units else 0

    def unit_of(ref, u):
        return ref.at[pl.ds(8 * (u // 2), 8), pl.ds(LANES * (u % 2), LANES)]

    def to_owner(u):
        return pltpu.make_async_remote_copy(
            src_ref=unit_of(mine, u), dst_ref=from_z.at[lot(u), z], send_sem=z_send.at[u],
            recv_sem=z_recv.at[lot(u), z], device_id={"clus": owner(u) * 2 + core},
            device_id_type=MESH,
        )

    for u in range(units):
        @pl.when(z != owner(u))
        def _():
            to_owner(u).start()

    def share(u, d):
        q = z_peer(d)
        return pltpu.make_async_remote_copy(
            src_ref=unit_of(done, u), dst_ref=unit_of(done, u), send_sem=zb_send.at[lot(u), q],
            recv_sem=zb_recv.at[u], device_id={"clus": q * 2 + core}, device_id_type=MESH,
        )

    for u in range(units):
        @pl.when(z == owner(u))
        def _():
            def gather(d, partial):
                q = z_peer(d)
                pltpu.make_async_remote_copy(
                    src_ref=unit_of(mine, u), dst_ref=from_z.at[lot(u), q],
                    send_sem=z_send.at[u], recv_sem=z_recv.at[lot(u), q],
                    device_id={"clus": q * 2 + core}, device_id_type=MESH,
                ).wait_recv()
                return partial + from_z[lot(u), q]

            unit_of(done, u)[...] = lax.fori_loop(1, depth, gather, unit_of(mine, u)[...])

            @pl.loop(1, depth)
            def _(d):
                share(u, d).start()

    for u in range(units):
        @pl.when(z != owner(u))
        def _():
            to_owner(u).wait_send()
            share(u, 1).wait_recv()

    def publish(p, slot):
        return pltpu.make_async_remote_copy(
            src_ref=final, dst_ref=total.at[core, slot], send_sem=r_send.at[p],
            recv_sem=r_recv.at[slot], device_id={"grp": p}, device_id_type=MESH,
        )

    def forward(half, p):
        return pltpu.make_async_remote_copy(
            src_ref=total.at[half, p], dst_ref=total.at[half, p], send_sem=w_send.at[p],
            recv_sem=w_recv.at[p], device_id={"clus": sibling}, device_id_type=MESH,
        )

    final[...] = done[...].astype(BF16)

    for p in peers:
        publish(p, g).start()

    total[core, g] = final[...]
    forward(core, g).start()

    @pl.loop(1, groups)
    def _(d):
        b_whole(grp_peer(d)).wait_recv()

    @pl.loop(0, slots)
    def _(i):
        fold[i] = came[i].astype(F32) + fold[tab[t_qprev + i]]

    @pl.loop(0, NB)
    def _(j):
        o_aux[pl.ds(j * BLK, BLK), :] = fold[tab[t_qlast + j]].astype(BF16)

    keeps[2].start()

    @pl.loop(1, groups)
    def _(d):
        p = grp_peer(d)
        publish(p, p).wait_recv()
        forward(core, p).start()

    @pl.loop(0, groups)
    def _(p):
        forward(1 - core, p).wait_recv()

    keeps[3].start()

    @pl.loop(1, groups)
    def _(d):
        h_whole(grp_peer(d)).wait_send()
        b_whole(grp_peer(d)).wait_send()
        spread_out(grp_peer(d)).wait_send()
        publish(grp_peer(d), g).wait_send()

    @pl.loop(0, groups)
    def _(p):
        forward(core, p).wait_send()

    for u in range(units):
        @pl.when(z == owner(u))
        def _():
            @pl.loop(1, depth)
            def _(d):
                share(u, d).wait_send()

    for keep in keeps:
        keep.wait()


def tail_kernel(groups, x_hist, x_hidden, x_aux, x_total,
                o_hist, o_hidden, o_aux, o_nf, o_sf, o_ns, o_ss, o_hz, o_loss,
                v_hist, v_hidden, v_aux, total, grads, into, out):
    rows_of = D // groups
    first = [
        pltpu.make_async_copy(a, b, into.at[i])
        for i, (a, b) in enumerate(
            ((x_total, total), (x_hist, v_hist), (x_hidden, v_hidden), (x_aux, v_aux))
        )
    ]
    second = [
        pltpu.make_async_copy(a, b, out.at[i])
        for i, (a, b) in enumerate(
            ((v_hist, o_hist), (v_hidden, o_hidden), (v_aux, o_aux), (grads.at[0], o_nf),
             (grads.at[1], o_sf), (grads.at[2], o_ns), (grads.at[3], o_ss))
        )
    ]
    for copy in first:
        copy.start()
    for t in range(1, 4):
        first[t].wait()
        second[t - 1].start()
    first[0].wait()
    for t, (half, base) in enumerate(((0, 0), (1, 0), (0, rows_of), (1, rows_of))):
        grads[t] = total[half, :, pl.ds(base, rows_of), :].astype(F32).reshape(D, D)
        second[3 + t].start()
    for t in range(TB // 8):
        o_hz[pl.ds(t * 8, 8), :] = total[t // 2, t % 2, pl.ds(2 * rows_of, 8), :].astype(F32)
    o_loss[...] = total[0, 2, pl.ds(2 * rows_of, 8), pl.ds(0, LANES)].astype(F32)[0:1, 0:1]
    for copy in second:
        copy.wait()


def latest(hit):
    count = hit.shape[1]
    place = lax.broadcasted_iota(jnp.int32, hit.shape, 1)
    found = jnp.max(jnp.where(hit, place, -1), axis=1)
    return jnp.where(found < 0, count, found)


def before(keys):
    shape = (keys.shape[0], keys.shape[0])
    earlier = lax.broadcasted_iota(jnp.int32, shape, 1) < lax.broadcasted_iota(jnp.int32, shape, 0)
    return latest((keys[None, :] == keys[:, None]) & earlier)


def holder(keys, count):
    return latest(keys[None, :] == lax.broadcasted_iota(jnp.int32, (count, keys.shape[0]), 0))


def shards(
    features, history, aux_history, tile_values, tile_sources, send_list, event_bins, event_flags,
    neigh_first, self_first, neigh_second, self_second, hazard_weight,
):
    groups = lax.axis_size("grp")
    depth = lax.axis_size("clus") // 2
    slots = groups * S
    rows_of = D // groups
    piece = 2 * rows_of + 8
    units = piece // 4
    lots = units if depth < units else 1
    src = tile_sources.reshape(TILES)
    snd = send_list.reshape(slots)
    tab = jnp.concatenate(
        [
            src, jnp.minimum(snd, NB - 1), before(src), holder(src, NB + slots), before(snd),
            holder(snd, NB),
        ]
    )
    any_spec = pl.BlockSpec(memory_space=pl.ANY)
    vmem = pl.BlockSpec(memory_space=pltpu.VMEM)
    dma = pltpu.SemaphoreType.DMA
    nodes = NB * BLK
    nodes_out = jax.ShapeDtypeStruct((nodes, D), BF16)
    weight_out = jax.ShapeDtypeStruct((D, D), F32)
    total_out = jax.ShapeDtypeStruct((2, groups, piece, D), BF16)
    scratch = [
        pltpu.VMEM((nodes, D), BF16),
        pltpu.VMEM((nodes, D), BF16),
        pltpu.VMEM((nodes, D), BF16),
        pltpu.VMEM((CHUNKS, 1, ROWS), jnp.int32),
        pltpu.VMEM((CHUNKS, 1, ROWS), jnp.int32),
        pltpu.VMEM((D, D), BF16),
        pltpu.VMEM((D, D), BF16),
        pltpu.VMEM((D, D), BF16),
        pltpu.VMEM((D, D), BF16),
        pltpu.VMEM((TB, D), BF16),
        pltpu.VMEM((NB, BLK, D), BF16),
        pltpu.VMEM((NB, BLK, D), BF16),
        pltpu.VMEM((nodes, D), BF16),
        pltpu.VMEM((NB, K, BLK, BLK), BF16),
        pltpu.VMEM((NB, K * BLK, BLK), BF16),
        pltpu.VMEM((NB + slots, BLK, D), BF16),
        pltpu.VMEM((NB + slots, BLK, D), BF16),
        pltpu.VMEM((slots, BLK, D), BF16),
        pltpu.VMEM((slots, BLK, D), BF16),
        pltpu.VMEM((nodes, D), BF16),
        pltpu.VMEM((nodes, D), BF16),
        pltpu.VMEM((nodes, D), F32),
        pltpu.VMEM((nodes, D), BF16),
        pltpu.VMEM((nodes, D), BF16),
        pltpu.VMEM((nodes, D), BF16),
        pltpu.VMEM((TB, nodes), BF16),
        pltpu.VMEM((TILES + 1, BLK, D), F32),
        pltpu.VMEM((slots, BLK, D), BF16),
        pltpu.VMEM((slots + 1, BLK, D), F32),
        pltpu.VMEM((TB, ROWS), F32),
        pltpu.VMEM((2, groups, piece, D), F32),
        pltpu.VMEM((2, groups, piece, D), BF16),
        pltpu.VMEM((groups, piece, D), F32),
        pltpu.VMEM((groups, piece, D), BF16),
        pltpu.VMEM((groups, piece, D), F32),
        pltpu.VMEM((groups, piece, D), BF16),
        pltpu.VMEM((piece, D), F32),
        pltpu.VMEM((lots, depth, 8, LANES), F32),
        pltpu.VMEM((piece, D), F32),
        pltpu.VMEM((piece, D), BF16),
        dma((12,)),
        dma((groups,)), dma((groups,)), dma((groups,)), dma((groups,)), dma((groups,)),
        dma((groups,)),
        dma((2,)), dma((groups,)), dma((groups,)), dma((units,)), dma((lots, depth)),
        dma((lots, depth)), dma((units,)), dma((groups,)), dma((groups,)), dma((groups,)),
        dma((groups,)),
    ]
    outs = pl.pallas_call(
        functools.partial(program_kernel, groups, depth),
        out_shape=(nodes_out,) * 3 + (total_out,),
        in_specs=[pl.BlockSpec(memory_space=pltpu.SMEM)] + [any_spec] * 11,
        out_specs=(any_spec,) * 4,
        scratch_shapes=scratch,
        compiler_params=pltpu.CompilerParams(
            collective_id=0, has_side_effects=True, vmem_limit_bytes=56 << 20
        ),
    )(
        tab,
        features.reshape(NB, BLK, D),
        history.reshape(NB, BLK, D),
        aux_history.reshape(nodes, D),
        tile_values.reshape(NB, K, BLK, BLK),
        event_bins.reshape(CHUNKS, 1, ROWS),
        event_flags.reshape(CHUNKS, 1, ROWS),
        neigh_first, self_first, neigh_second, self_second, hazard_weight.T,
    )
    hist, hidden, aux, nf, sf, ns, ss, hz, loss = pl.pallas_call(
        functools.partial(tail_kernel, groups),
        out_shape=(nodes_out,) * 3 + (weight_out,) * 4 + (
            jax.ShapeDtypeStruct((TB, D), F32), jax.ShapeDtypeStruct((1, 1), F32),
        ),
        in_specs=[any_spec] * 4,
        out_specs=(any_spec,) * 7 + (vmem,) * 2,
        scratch_shapes=[
            pltpu.VMEM((nodes, D), BF16),
            pltpu.VMEM((nodes, D), BF16),
            pltpu.VMEM((nodes, D), BF16),
            pltpu.VMEM((2, groups, piece, D), BF16),
            pltpu.VMEM((4, D, D), F32),
            dma((4,)),
            dma((7,)),
        ],
        compiler_params=pltpu.CompilerParams(vmem_limit_bytes=58 << 20),
    )(*outs)
    return (
        hist[None, None], hidden[None, None], aux[None, None],
        nf, sf, ns, ss, hz.T, loss[0, 0],
    )


def solution(mesh):
    in_specs = (
        P("clus", "grp", None, None),
        P("clus", "grp", None, None),
        P("clus", "grp", None, None),
        P("clus", "grp", None, None, None, None),
        P("clus", "grp", None, None),
        P("clus", "grp", None, None),
        P("clus", "grp", None),
        P("clus", "grp", None),
        P(), P(), P(), P(), P(),
    )
    out_specs = (
        P("clus", "grp", None, None),
        P("clus", "grp", None, None),
        P("clus", "grp", None, None),
        P(), P(), P(), P(), P(), P(),
    )
    return jax.shard_map(shards, mesh=mesh, in_specs=in_specs, out_specs=out_specs, check_vma=False)
```

```python
import functools

import jax
import jax.numpy as jnp
from jax import lax
from jax.experimental import pallas as pl
from jax.experimental.pallas import tpu as pltpu
from jax.sharding import PartitionSpec as P

MESH = pl.DeviceIdType.MESH
F32 = jnp.float32
BF16 = jnp.bfloat16
NB = 8
K = 4
S = 2
BLK = 128
D = 256
TB = 32
TILES = NB * K
CHUNK = 2
ROWS = CHUNK * BLK
CHUNKS = NB // CHUNK
LANES = 128
PARTS = 4
PART = S * BLK // PARTS
ORDER = (
    (2, 2), (1, 0), (0, 1), (3, 0), (0, 3), (1, 1), (3, 3), (1, 3),
    (3, 1), (2, 0), (0, 2), (2, 1), (1, 2), (2, 3), (3, 2),
)


def nn(a, b):
    return jnp.dot(a, b, preferred_element_type=F32)


def nt(a, b):
    return lax.dot_general(a, b, (((1,), (1,)), ((), ())), preferred_element_type=F32)


def tn(a, b):
    return lax.dot_general(a, b, (((0,), (0,)), ((), ())), preferred_element_type=F32)


def sigmoid(v):
    return 0.5 * jnp.tanh(0.5 * v) + 0.5


def slope(v):
    q = sigmoid(v)
    return q * (1.0 + v * (1.0 - q))


def program_kernel(
    groups, depth,
    tab, feat_in, hist_in, aux_in, tiles_in, bins_in, flags_in, nf_in, sf_in, ns_in, ss_in, hz_in,
    x_hist, x_hidden, x_aux, x_total,
    o_hist, o_hidden, o_aux, bins, flags, w_nf, w_sf, w_ns, w_ss, w_hz,
    own, past, aux, tiles, turned, table1, table2, stage1, stage2, agg1, agg2, pre1, hid2, gp2,
    gp1, glog, chain, came, fold, loss_acc,
    pack, total, acc, narrow, from_core, from_grp, mine, from_z, done, final,
    load_sem, f_send, f_recv, h_send, h_recv, b_send, b_recv,
    core_sem, g_send, g_recv, z_send, z_recv, zb_send, zb_recv, r_send, r_recv, w_send, w_recv,
):
    slots = groups * S
    t_src = 0
    t_snd = t_src + TILES
    t_prev = t_snd + slots
    t_last = t_prev + TILES
    t_qprev = t_last + NB + slots
    t_qlast = t_qprev + slots
    rows_of = D // groups
    piece = 2 * rows_of + 8
    units = piece // 4
    scale = 1.0 / (NB * BLK * groups)

    clus = lax.axis_index("clus")
    g = lax.axis_index("grp")
    core = lax.rem(clus, 2)
    z = clus // 2
    sibling = clus + 1 - 2 * core

    def grp_peer(d):
        return lax.rem(g + d, groups)

    def z_peer(d):
        return lax.rem(z + d, depth)

    side = int(groups ** 0.5)
    gx = g // side
    gy = lax.rem(g, side)
    peers = [
        lax.rem(gx + dx, side) * side + lax.rem(gy + dy, side)
        for dx, dy in ORDER if dx < side and dy < side
    ]

    loads = [
        pltpu.make_async_copy(feat_in, own, load_sem.at[0]),
        pltpu.make_async_copy(hist_in, past, load_sem.at[1]),
        pltpu.make_async_copy(feat_in, table1.at[pl.ds(0, NB)], load_sem.at[2]),
        pltpu.make_async_copy(tiles_in, tiles, load_sem.at[3]),
        pltpu.make_async_copy(aux_in, aux, load_sem.at[4]),
        pltpu.make_async_copy(nf_in, w_nf, load_sem.at[5]),
        pltpu.make_async_copy(sf_in, w_sf, load_sem.at[6]),
        pltpu.make_async_copy(ns_in, w_ns, load_sem.at[7]),
        pltpu.make_async_copy(ss_in, w_ss, load_sem.at[8]),
        pltpu.make_async_copy(hz_in, w_hz, load_sem.at[9]),
        pltpu.make_async_copy(bins_in, bins, load_sem.at[10]),
        pltpu.make_async_copy(flags_in, flags, load_sem.at[11]),
    ]
    for load in loads:
        load.start()

    barrier = pltpu.get_barrier_semaphore()
    pl.semaphore_signal(barrier, inc=1, device_id={"clus": sibling}, device_id_type=MESH)

    @pl.loop(1, groups)
    def _(d):
        pl.semaphore_signal(barrier, inc=1, device_id={"grp": grp_peer(d)}, device_id_type=MESH)

    @pl.loop(1, depth)
    def _(d):
        pl.semaphore_signal(
            barrier, inc=1, device_id={"clus": z_peer(d) * 2 + core}, device_id_type=MESH
        )

    blank = jnp.zeros((S, BLK, D), BF16)
    table1[pl.ds(NB + g * S, S)] = blank
    table2[pl.ds(NB + g * S, S)] = blank
    came[pl.ds(g * S, S)] = blank
    chain[TILES] = jnp.zeros((BLK, D), F32)
    fold[slots] = jnp.zeros((BLK, D), F32)
    pack[:, :, 2 * rows_of :, :] = jnp.zeros((2, groups, 8, D), F32)

    pl.semaphore_wait(barrier, groups + depth - 1)

    def exchange(stage, target, base, send, recv):
        def out(p, part):
            s = part * PART // BLK
            rows = pl.ds(pl.multiple_of(lax.rem(part * PART, BLK), PART), PART)
            return pltpu.make_async_remote_copy(
                src_ref=stage.at[p * S + s, rows], dst_ref=target.at[base + g * S + s, rows],
                send_sem=send.at[p], recv_sem=recv.at[g],
                device_id={"grp": p}, device_id_type=MESH,
            )

        def whole(p):
            return pltpu.make_async_remote_copy(
                src_ref=stage.at[pl.ds(p * S, S)], dst_ref=target.at[pl.ds(base + p * S, S)],
                send_sem=send.at[p], recv_sem=recv.at[p],
                device_id={"grp": p}, device_id_type=MESH,
            )

        def post(load, first, last):
            @pl.loop(first, last)
            def _(part):
                s = part * PART // BLK
                rows = pl.ds(pl.multiple_of(lax.rem(part * PART, BLK), PART), PART)
                for p in peers:
                    stage[p * S + s, rows] = load(p * S + s, rows).astype(BF16)
                    out(p, part).start()

        return post, whole

    f_post, f_whole = exchange(stage1, table1, NB, f_send, f_recv)
    h_post, h_whole = exchange(stage2, table2, NB, h_send, h_recv)
    b_post, b_whole = exchange(stage1, came, 0, b_send, b_recv)

    loads[0].wait()
    f_post(lambda q, rows: own[tab[t_snd + q], rows], 0, PARTS)
    loads[1].wait()
    h_post(lambda q, rows: past[tab[t_snd + q], rows], 0, PARTS)

    loads[3].wait()

    @pl.loop(0, NB)
    def _(b):
        for k in range(K):
            turned[b, pl.ds(k * BLK, BLK), :] = tiles[b, k].T

    for load in loads[4:] + loads[2:3]:
        load.wait()

    @pl.loop(1, groups)
    def _(d):
        f_whole(grp_peer(d)).wait()

    def aggregate(table, b):
        wide = jnp.concatenate([tiles[b, k] for k in range(K)], axis=1)
        deep = jnp.concatenate([table[tab[t_src + b * K + k]] for k in range(K)], axis=0)
        return nn(wide, deep).astype(BF16)

    @pl.loop(0, CHUNKS)
    def _(c):
        a = jnp.concatenate([aggregate(table1, c * CHUNK + j) for j in range(CHUNK)], axis=0)
        rows = pl.ds(pl.multiple_of(c * ROWS, ROWS), ROWS)
        blocks = pl.ds(c * CHUNK, CHUNK)
        agg1[rows, :] = a
        pre = nn(a, w_nf[...]) + nn(own[blocks].reshape(ROWS, D), w_sf[...])
        pre1[rows, :] = pre
        h = (pre * sigmoid(pre)).astype(BF16)
        table2[blocks] = h.reshape(CHUNK, BLK, D)
        o_hist[rows, :] = h

    keeps = [
        pltpu.make_async_copy(o_hist, x_hist, load_sem.at[0]),
        pltpu.make_async_copy(o_hidden, x_hidden, load_sem.at[1]),
        pltpu.make_async_copy(o_aux, x_aux, load_sem.at[2]),
        pltpu.make_async_copy(total, x_total, load_sem.at[3]),
    ]
    keeps[0].start()
    loss_acc[...] = jnp.zeros((TB, ROWS), F32)

    @pl.loop(1, groups)
    def _(d):
        h_whole(grp_peer(d)).wait_recv()

    @pl.loop(0, CHUNKS)
    def _(c):
        a = jnp.concatenate([aggregate(table2, c * CHUNK + j) for j in range(CHUNK)], axis=0)
        rows = pl.ds(pl.multiple_of(c * ROWS, ROWS), ROWS)
        blocks = pl.ds(c * CHUNK, CHUNK)
        agg2[rows, :] = a
        pre = nn(a, w_ns[...]) + nn(table2[blocks].reshape(ROWS, D), w_ss[...])
        q = sigmoid(pre)
        h = (pre * q).astype(BF16)
        hid2[rows, :] = h
        logits = nt(w_hz[...], h)
        step = lax.broadcasted_iota(jnp.int32, (TB, ROWS), 0)
        bin_row = bins[c]
        flag_row = flags[c].astype(F32)
        counted = step <= bin_row
        event = jnp.where(step == bin_row, flag_row, 0.0)
        soft = jnp.maximum(logits, 0.0) + jnp.log1p(jnp.exp(-jnp.abs(logits)))
        loss_acc[...] += jnp.where(counted, soft, 0.0) - event * logits
        gl = (jnp.where(counted, sigmoid(logits), 0.0) - event).astype(BF16)
        glog[:, rows] = gl
        gp = (tn(gl, w_hz[...]) * (q * (1.0 + pre * (1.0 - q)))).astype(BF16)
        gp2[rows, :] = gp
        ga = nt(gp, w_ns[...]).astype(BF16)
        for j in range(CHUNK):
            b = c * CHUNK + j
            spread = nn(turned[b], ga[j * BLK : (j + 1) * BLK])
            for k in range(K):
                i = b * K + k
                chain[i] = spread[k * BLK : (k + 1) * BLK] + chain[tab[t_prev + i]]

    def returned(q, rows):
        return chain[tab[t_last + NB + q], rows]

    b_post(returned, 0, PARTS // 4)

    def put(half, base, value):
        pack[half, :, pl.ds(base, rows_of), :] = (value * scale).reshape(groups, rows_of, D)

    put(0, rows_of, tn(agg2[...], gp2[...]))
    put(1, rows_of, tn(table2[pl.ds(0, NB)].reshape(NB * BLK, D), gp2[...]))
    hz = nn(glog[...], hid2[...]) * scale
    for t in range(TB // 8):
        pack[t // 2, t % 2, pl.ds(2 * rows_of, 8), :] = hz[t * 8 : (t + 1) * 8]
    loss = jnp.sum(loss_acc[...], keepdims=True) * scale
    pack[0, 2, pl.ds(2 * rows_of, 8), :] = jnp.broadcast_to(loss, (8, D))

    @pl.loop(0, CHUNKS)
    def _(c):
        rows = pl.ds(pl.multiple_of(c * ROWS, ROWS), ROWS)
        local = jnp.concatenate(
            [chain[tab[t_last + c * CHUNK + j]] for j in range(CHUNK)], axis=0
        )
        grad = local + nt(gp2[rows, :], w_ss[...]) + aux[rows, :].astype(F32)
        o_hidden[rows, :] = grad.astype(BF16)
        gp1[rows, :] = (grad * slope(pre1[rows, :])).astype(BF16)

    keeps[1].start()
    put(0, 0, tn(agg1[...], gp1[...]))
    put(1, 0, tn(own[...].reshape(NB * BLK, D), gp1[...]))

    swap = pltpu.make_async_remote_copy(
        src_ref=pack.at[1 - core], dst_ref=from_core, send_sem=core_sem.at[0],
        recv_sem=core_sem.at[1], device_id={"clus": sibling}, device_id_type=MESH,
    )
    swap.start()

    swap.wait()
    acc[...] = pack[core] + from_core[...]
    narrow[...] = acc[...].astype(BF16)

    def spread_out(p):
        return pltpu.make_async_remote_copy(
            src_ref=narrow.at[p], dst_ref=from_grp.at[g], send_sem=g_send.at[p],
            recv_sem=g_recv.at[g], device_id={"grp": p}, device_id_type=MESH,
        )

    for p in peers:
        spread_out(p).start()

    b_post(returned, PARTS // 4, PARTS)

    mine[...] = acc[g]

    @pl.loop(1, groups)
    def _(d):
        p = grp_peer(d)
        pltpu.make_async_remote_copy(
            src_ref=narrow.at[p], dst_ref=from_grp.at[p], send_sem=g_send.at[p],
            recv_sem=g_recv.at[p], device_id={"grp": p}, device_id_type=MESH,
        ).wait_recv()
        mine[...] += from_grp[p].astype(F32)

    def owner(u):
        return (u * depth) // units

    def lot(u):
        return u if depth < units else 0

    def unit_of(ref, u):
        return ref.at[pl.ds(8 * (u // 2), 8), pl.ds(LANES * (u % 2), LANES)]

    def to_owner(u):
        return pltpu.make_async_remote_copy(
            src_ref=unit_of(mine, u), dst_ref=from_z.at[lot(u), z], send_sem=z_send.at[u],
            recv_sem=z_recv.at[lot(u), z], device_id={"clus": owner(u) * 2 + core},
            device_id_type=MESH,
        )

    for u in range(units):
        @pl.when(z != owner(u))
        def _():
            to_owner(u).start()

    def share(u, d):
        q = z_peer(d)
        return pltpu.make_async_remote_copy(
            src_ref=unit_of(done, u), dst_ref=unit_of(done, u), send_sem=zb_send.at[lot(u), q],
            recv_sem=zb_recv.at[u], device_id={"clus": q * 2 + core}, device_id_type=MESH,
        )

    for u in range(units):
        @pl.when(z == owner(u))
        def _():
            def gather(d, partial):
                q = z_peer(d)
                pltpu.make_async_remote_copy(
                    src_ref=unit_of(mine, u), dst_ref=from_z.at[lot(u), q],
                    send_sem=z_send.at[u], recv_sem=z_recv.at[lot(u), q],
                    device_id={"clus": q * 2 + core}, device_id_type=MESH,
                ).wait_recv()
                return partial + from_z[lot(u), q]

            unit_of(done, u)[...] = lax.fori_loop(1, depth, gather, unit_of(mine, u)[...])

            @pl.loop(1, depth)
            def _(d):
                share(u, d).start()

    for u in range(units):
        @pl.when(z != owner(u))
        def _():
            to_owner(u).wait_send()
            share(u, 1).wait_recv()

    def publish(p, slot):
        return pltpu.make_async_remote_copy(
            src_ref=final, dst_ref=total.at[core, slot], send_sem=r_send.at[p],
            recv_sem=r_recv.at[slot], device_id={"grp": p}, device_id_type=MESH,
        )

    def forward(half, p):
        return pltpu.make_async_remote_copy(
            src_ref=total.at[half, p], dst_ref=total.at[half, p], send_sem=w_send.at[p],
            recv_sem=w_recv.at[p], device_id={"clus": sibling}, device_id_type=MESH,
        )

    final[...] = done[...].astype(BF16)

    for p in peers:
        publish(p, g).start()

    total[core, g] = final[...]
    forward(core, g).start()

    @pl.loop(1, groups)
    def _(d):
        b_whole(grp_peer(d)).wait_recv()

    @pl.loop(0, slots)
    def _(i):
        fold[i] = came[i].astype(F32) + fold[tab[t_qprev + i]]

    @pl.loop(0, NB)
    def _(j):
        o_aux[pl.ds(j * BLK, BLK), :] = fold[tab[t_qlast + j]].astype(BF16)

    keeps[2].start()

    @pl.loop(1, groups)
    def _(d):
        p = grp_peer(d)
        publish(p, p).wait_recv()
        forward(core, p).start()

    @pl.loop(0, groups)
    def _(p):
        forward(1 - core, p).wait_recv()

    keeps[3].start()

    @pl.loop(1, groups)
    def _(d):
        h_whole(grp_peer(d)).wait_send()
        b_whole(grp_peer(d)).wait_send()
        spread_out(grp_peer(d)).wait_send()
        publish(grp_peer(d), g).wait_send()

    @pl.loop(0, groups)
    def _(p):
        forward(core, p).wait_send()

    for u in range(units):
        @pl.when(z == owner(u))
        def _():
            @pl.loop(1, depth)
            def _(d):
                share(u, d).wait_send()

    for keep in keeps:
        keep.wait()


def tail_kernel(groups, x_hist, x_hidden, x_aux, x_total,
                o_hist, o_hidden, o_aux, o_nf, o_sf, o_ns, o_ss, o_hz, o_loss,
                v_hist, v_hidden, v_aux, total, grads, into, out):
    rows_of = D // groups
    first = [
        pltpu.make_async_copy(a, b, into.at[i])
        for i, (a, b) in enumerate(
            ((x_total, total), (x_hist, v_hist), (x_hidden, v_hidden), (x_aux, v_aux))
        )
    ]
    second = [
        pltpu.make_async_copy(a, b, out.at[i])
        for i, (a, b) in enumerate(
            ((v_hist, o_hist), (v_hidden, o_hidden), (v_aux, o_aux), (grads.at[0], o_nf),
             (grads.at[1], o_sf), (grads.at[2], o_ns), (grads.at[3], o_ss))
        )
    ]
    for copy in first:
        copy.start()
    for t in range(1, 4):
        first[t].wait()
        second[t - 1].start()
    first[0].wait()
    for t, (half, base) in enumerate(((0, 0), (1, 0), (0, rows_of), (1, rows_of))):
        grads[t] = total[half, :, pl.ds(base, rows_of), :].astype(F32).reshape(D, D)
        second[3 + t].start()
    for t in range(TB // 8):
        o_hz[pl.ds(t * 8, 8), :] = total[t // 2, t % 2, pl.ds(2 * rows_of, 8), :].astype(F32)
    o_loss[...] = total[0, 2, pl.ds(2 * rows_of, 8), pl.ds(0, LANES)].astype(F32)[0:1, 0:1]
    for copy in second:
        copy.wait()


def latest(hit):
    count = hit.shape[1]
    place = lax.broadcasted_iota(jnp.int32, hit.shape, 1)
    found = jnp.max(jnp.where(hit, place, -1), axis=1)
    return jnp.where(found < 0, count, found)


def before(keys):
    shape = (keys.shape[0], keys.shape[0])
    earlier = lax.broadcasted_iota(jnp.int32, shape, 1) < lax.broadcasted_iota(jnp.int32, shape, 0)
    return latest((keys[None, :] == keys[:, None]) & earlier)


def holder(keys, count):
    return latest(keys[None, :] == lax.broadcasted_iota(jnp.int32, (count, keys.shape[0]), 0))


def shards(
    features, history, aux_history, tile_values, tile_sources, send_list, event_bins, event_flags,
    neigh_first, self_first, neigh_second, self_second, hazard_weight,
):
    groups = lax.axis_size("grp")
    depth = lax.axis_size("clus") // 2
    slots = groups * S
    rows_of = D // groups
    piece = 2 * rows_of + 8
    units = piece // 4
    lots = units if depth < units else 1
    src = tile_sources.reshape(TILES)
    snd = send_list.reshape(slots)
    tab = jnp.concatenate(
        [
            src, jnp.minimum(snd, NB - 1), before(src), holder(src, NB + slots), before(snd),
            holder(snd, NB),
        ]
    )
    any_spec = pl.BlockSpec(memory_space=pl.ANY)
    vmem = pl.BlockSpec(memory_space=pltpu.VMEM)
    dma = pltpu.SemaphoreType.DMA
    nodes = NB * BLK
    nodes_out = jax.ShapeDtypeStruct((nodes, D), BF16)
    weight_out = jax.ShapeDtypeStruct((D, D), F32)
    total_out = jax.ShapeDtypeStruct((2, groups, piece, D), BF16)
    scratch = [
        pltpu.VMEM((nodes, D), BF16),
        pltpu.VMEM((nodes, D), BF16),
        pltpu.VMEM((nodes, D), BF16),
        pltpu.VMEM((CHUNKS, 1, ROWS), jnp.int32),
        pltpu.VMEM((CHUNKS, 1, ROWS), jnp.int32),
        pltpu.VMEM((D, D), BF16),
        pltpu.VMEM((D, D), BF16),
        pltpu.VMEM((D, D), BF16),
        pltpu.VMEM((D, D), BF16),
        pltpu.VMEM((TB, D), BF16),
        pltpu.VMEM((NB, BLK, D), BF16),
        pltpu.VMEM((NB, BLK, D), BF16),
        pltpu.VMEM((nodes, D), BF16),
        pltpu.VMEM((NB, K, BLK, BLK), BF16),
        pltpu.VMEM((NB, K * BLK, BLK), BF16),
        pltpu.VMEM((NB + slots, BLK, D), BF16),
        pltpu.VMEM((NB + slots, BLK, D), BF16),
        pltpu.VMEM((slots, BLK, D), BF16),
        pltpu.VMEM((slots, BLK, D), BF16),
        pltpu.VMEM((nodes, D), BF16),
        pltpu.VMEM((nodes, D), BF16),
        pltpu.VMEM((nodes, D), F32),
        pltpu.VMEM((nodes, D), BF16),
        pltpu.VMEM((nodes, D), BF16),
        pltpu.VMEM((nodes, D), BF16),
        pltpu.VMEM((TB, nodes), BF16),
        pltpu.VMEM((TILES + 1, BLK, D), F32),
        pltpu.VMEM((slots, BLK, D), BF16),
        pltpu.VMEM((slots + 1, BLK, D), F32),
        pltpu.VMEM((TB, ROWS), F32),
        pltpu.VMEM((2, groups, piece, D), F32),
        pltpu.VMEM((2, groups, piece, D), BF16),
        pltpu.VMEM((groups, piece, D), F32),
        pltpu.VMEM((groups, piece, D), BF16),
        pltpu.VMEM((groups, piece, D), F32),
        pltpu.VMEM((groups, piece, D), BF16),
        pltpu.VMEM((piece, D), F32),
        pltpu.VMEM((lots, depth, 8, LANES), F32),
        pltpu.VMEM((piece, D), F32),
        pltpu.VMEM((piece, D), BF16),
        dma((12,)),
        dma((groups,)), dma((groups,)), dma((groups,)), dma((groups,)), dma((groups,)),
        dma((groups,)),
        dma((2,)), dma((groups,)), dma((groups,)), dma((units,)), dma((lots, depth)),
        dma((lots, depth)), dma((units,)), dma((groups,)), dma((groups,)), dma((groups,)),
        dma((groups,)),
    ]
    outs = pl.pallas_call(
        functools.partial(program_kernel, groups, depth),
        out_shape=(nodes_out,) * 3 + (total_out,),
        in_specs=[pl.BlockSpec(memory_space=pltpu.SMEM)] + [any_spec] * 11,
        out_specs=(any_spec,) * 4,
        scratch_shapes=scratch,
        compiler_params=pltpu.CompilerParams(
            collective_id=0, has_side_effects=True, vmem_limit_bytes=56 << 20
        ),
    )(
        tab,
        features.reshape(NB, BLK, D),
        history.reshape(NB, BLK, D),
        aux_history.reshape(nodes, D),
        tile_values.reshape(NB, K, BLK, BLK),
        event_bins.reshape(CHUNKS, 1, ROWS),
        event_flags.reshape(CHUNKS, 1, ROWS),
        neigh_first, self_first, neigh_second, self_second, hazard_weight.T,
    )
    hist, hidden, aux, nf, sf, ns, ss, hz, loss = pl.pallas_call(
        functools.partial(tail_kernel, groups),
        out_shape=(nodes_out,) * 3 + (weight_out,) * 4 + (
            jax.ShapeDtypeStruct((TB, D), F32), jax.ShapeDtypeStruct((1, 1), F32),
        ),
        in_specs=[any_spec] * 4,
        out_specs=(any_spec,) * 7 + (vmem,) * 2,
        scratch_shapes=[
            pltpu.VMEM((nodes, D), BF16),
            pltpu.VMEM((nodes, D), BF16),
            pltpu.VMEM((nodes, D), BF16),
            pltpu.VMEM((2, groups, piece, D), BF16),
            pltpu.VMEM((4, D, D), F32),
            dma((4,)),
            dma((7,)),
        ],
        compiler_params=pltpu.CompilerParams(vmem_limit_bytes=58 << 20),
    )(*outs)
    return (
        hist[None, None], hidden[None, None], aux[None, None],
        nf, sf, ns, ss, hz.T, loss[0, 0],
    )


def solution(mesh):
    in_specs = (
        P("clus", "grp", None, None),
        P("clus", "grp", None, None),
        P("clus", "grp", None, None),
        P("clus", "grp", None, None, None, None),
        P("clus", "grp", None, None),
        P("clus", "grp", None, None),
        P("clus", "grp", None),
        P("clus", "grp", None),
        P(), P(), P(), P(), P(),
    )
    out_specs = (
        P("clus", "grp", None, None),
        P("clus", "grp", None, None),
        P("clus", "grp", None, None),
        P(), P(), P(), P(), P(), P(),
    )
    return jax.shard_map(shards, mesh=mesh, in_specs=in_specs, out_specs=out_specs, check_vma=False)
```

```python
import functools

import jax
import jax.numpy as jnp
from jax import lax
from jax.experimental import pallas as pl
from jax.experimental.pallas import tpu as pltpu
from jax.sharding import PartitionSpec as P

MESH = pl.DeviceIdType.MESH
F32 = jnp.float32
BF16 = jnp.bfloat16
NB = 8
K = 4
S = 2
BLK = 128
D = 256
TB = 32
TILES = NB * K
CHUNK = 2
ROWS = CHUNK * BLK
CHUNKS = NB // CHUNK
LANES = 128
PARTS = 4
PART = S * BLK // PARTS
ORDER = (
    (2, 2), (1, 0), (0, 1), (3, 0), (0, 3), (1, 1), (3, 3), (1, 3),
    (3, 1), (2, 0), (0, 2), (2, 1), (1, 2), (2, 3), (3, 2),
)


def nn(a, b):
    return jnp.dot(a, b, preferred_element_type=F32)


def nt(a, b):
    return lax.dot_general(a, b, (((1,), (1,)), ((), ())), preferred_element_type=F32)


def tn(a, b):
    return lax.dot_general(a, b, (((0,), (0,)), ((), ())), preferred_element_type=F32)


def sigmoid(v):
    return 0.5 * jnp.tanh(0.5 * v) + 0.5


def slope(v):
    q = sigmoid(v)
    return q * (1.0 + v * (1.0 - q))


def program_kernel(
    groups, depth,
    tab, feat_in, hist_in, aux_in, tiles_in, bins_in, flags_in, nf_in, sf_in, ns_in, ss_in, hz_in,
    x_hist, x_hidden, x_aux, x_total,
    o_hist, o_hidden, o_aux, bins, flags, w_nf, w_sf, w_ns, w_ss, w_hz,
    own, past, aux, tiles, turned, table1, table2, stage1, stage2, agg1, agg2, pre1, hid2, gp2,
    gp1, glog, chain, came, fold, loss_acc,
    pack, total, acc, narrow, from_core, from_grp, mine, from_z, done, final,
    load_sem, f_send, f_recv, h_send, h_recv, b_send, b_recv,
    core_sem, g_send, g_recv, z_send, z_recv, zb_send, zb_recv, r_send, r_recv, w_send, w_recv,
):
    slots = groups * S
    t_src = 0
    t_snd = t_src + TILES
    t_prev = t_snd + slots
    t_last = t_prev + TILES
    t_qprev = t_last + NB + slots
    t_qlast = t_qprev + slots
    rows_of = D // groups
    piece = 2 * rows_of + 8
    units = piece // 4
    scale = 1.0 / (NB * BLK * groups)

    clus = lax.axis_index("clus")
    g = lax.axis_index("grp")
    core = lax.rem(clus, 2)
    z = clus // 2
    sibling = clus + 1 - 2 * core

    def grp_peer(d):
        return lax.rem(g + d, groups)

    def z_peer(d):
        return lax.rem(z + d, depth)

    side = int(groups ** 0.5)
    gx = g // side
    gy = lax.rem(g, side)
    peers = [
        lax.rem(gx + dx, side) * side + lax.rem(gy + dy, side)
        for dx, dy in ORDER if dx < side and dy < side
    ]

    loads = [
        pltpu.make_async_copy(feat_in, own, load_sem.at[0]),
        pltpu.make_async_copy(hist_in, past, load_sem.at[1]),
        pltpu.make_async_copy(feat_in, table1.at[pl.ds(0, NB)], load_sem.at[2]),
        pltpu.make_async_copy(tiles_in, tiles, load_sem.at[3]),
        pltpu.make_async_copy(aux_in, aux, load_sem.at[4]),
        pltpu.make_async_copy(nf_in, w_nf, load_sem.at[5]),
        pltpu.make_async_copy(sf_in, w_sf, load_sem.at[6]),
        pltpu.make_async_copy(ns_in, w_ns, load_sem.at[7]),
        pltpu.make_async_copy(ss_in, w_ss, load_sem.at[8]),
        pltpu.make_async_copy(hz_in, w_hz, load_sem.at[9]),
        pltpu.make_async_copy(bins_in, bins, load_sem.at[10]),
        pltpu.make_async_copy(flags_in, flags, load_sem.at[11]),
    ]
    for load in loads:
        load.start()

    barrier = pltpu.get_barrier_semaphore()
    pl.semaphore_signal(barrier, inc=1, device_id={"clus": sibling}, device_id_type=MESH)

    @pl.loop(1, groups)
    def _(d):
        pl.semaphore_signal(barrier, inc=1, device_id={"grp": grp_peer(d)}, device_id_type=MESH)

    @pl.loop(1, depth)
    def _(d):
        pl.semaphore_signal(
            barrier, inc=1, device_id={"clus": z_peer(d) * 2 + core}, device_id_type=MESH
        )

    blank = jnp.zeros((S, BLK, D), BF16)
    table1[pl.ds(NB + g * S, S)] = blank
    table2[pl.ds(NB + g * S, S)] = blank
    came[pl.ds(g * S, S)] = blank
    chain[TILES] = jnp.zeros((BLK, D), F32)
    fold[slots] = jnp.zeros((BLK, D), F32)
    pack[:, :, 2 * rows_of :, :] = jnp.zeros((2, groups, 8, D), F32)

    pl.semaphore_wait(barrier, groups + depth - 1)

    def exchange(stage, target, base, send, recv):
        def out(p, part):
            s = part * PART // BLK
            rows = pl.ds(pl.multiple_of(lax.rem(part * PART, BLK), PART), PART)
            return pltpu.make_async_remote_copy(
                src_ref=stage.at[p * S + s, rows], dst_ref=target.at[base + g * S + s, rows],
                send_sem=send.at[p], recv_sem=recv.at[g],
                device_id={"grp": p}, device_id_type=MESH,
            )

        def whole(p):
            return pltpu.make_async_remote_copy(
                src_ref=stage.at[pl.ds(p * S, S)], dst_ref=target.at[pl.ds(base + p * S, S)],
                send_sem=send.at[p], recv_sem=recv.at[p],
                device_id={"grp": p}, device_id_type=MESH,
            )

        def post(load, first, last):
            @pl.loop(first, last)
            def _(part):
                s = part * PART // BLK
                rows = pl.ds(pl.multiple_of(lax.rem(part * PART, BLK), PART), PART)
                for p in peers:
                    stage[p * S + s, rows] = load(p * S + s, rows).astype(BF16)
                    out(p, part).start()

        return post, whole

    f_post, f_whole = exchange(stage1, table1, NB, f_send, f_recv)
    h_post, h_whole = exchange(stage2, table2, NB, h_send, h_recv)
    b_post, b_whole = exchange(stage1, came, 0, b_send, b_recv)

    loads[0].wait()
    f_post(lambda q, rows: own[tab[t_snd + q], rows], 0, PARTS)
    loads[1].wait()
    h_post(lambda q, rows: past[tab[t_snd + q], rows], 0, PARTS)

    loads[3].wait()

    @pl.loop(0, NB)
    def _(b):
        for k in range(K):
            turned[b, pl.ds(k * BLK, BLK), :] = tiles[b, k].T

    for load in loads[4:] + loads[2:3]:
        load.wait()

    @pl.loop(1, groups)
    def _(d):
        f_whole(grp_peer(d)).wait()

    def aggregate(table, b):
        wide = jnp.concatenate([tiles[b, k] for k in range(K)], axis=1)
        deep = jnp.concatenate([table[tab[t_src + b * K + k]] for k in range(K)], axis=0)
        return nn(wide, deep).astype(BF16)

    @pl.loop(0, CHUNKS)
    def _(c):
        a = jnp.concatenate([aggregate(table1, c * CHUNK + j) for j in range(CHUNK)], axis=0)
        rows = pl.ds(pl.multiple_of(c * ROWS, ROWS), ROWS)
        blocks = pl.ds(c * CHUNK, CHUNK)
        agg1[rows, :] = a
        pre = nn(a, w_nf[...]) + nn(own[blocks].reshape(ROWS, D), w_sf[...])
        pre1[rows, :] = pre
        h = (pre * sigmoid(pre)).astype(BF16)
        table2[blocks] = h.reshape(CHUNK, BLK, D)
        o_hist[rows, :] = h

    keeps = [
        pltpu.make_async_copy(o_hist, x_hist, load_sem.at[0]),
        pltpu.make_async_copy(o_hidden, x_hidden, load_sem.at[1]),
        pltpu.make_async_copy(o_aux, x_aux, load_sem.at[2]),
        pltpu.make_async_copy(total, x_total, load_sem.at[3]),
    ]
    keeps[0].start()
    loss_acc[...] = jnp.zeros((TB, ROWS), F32)

    @pl.loop(1, groups)
    def _(d):
        h_whole(grp_peer(d)).wait_recv()

    @pl.loop(0, CHUNKS)
    def _(c):
        a = jnp.concatenate([aggregate(table2, c * CHUNK + j) for j in range(CHUNK)], axis=0)
        rows = pl.ds(pl.multiple_of(c * ROWS, ROWS), ROWS)
        blocks = pl.ds(c * CHUNK, CHUNK)
        agg2[rows, :] = a
        pre = nn(a, w_ns[...]) + nn(table2[blocks].reshape(ROWS, D), w_ss[...])
        q = sigmoid(pre)
        h = (pre * q).astype(BF16)
        hid2[rows, :] = h
        logits = nt(w_hz[...], h)
        step = lax.broadcasted_iota(jnp.int32, (TB, ROWS), 0)
        bin_row = bins[c]
        flag_row = flags[c].astype(F32)
        counted = step <= bin_row
        event = jnp.where(step == bin_row, flag_row, 0.0)
        soft = jnp.maximum(logits, 0.0) + jnp.log1p(jnp.exp(-jnp.abs(logits)))
        loss_acc[...] += jnp.where(counted, soft, 0.0) - event * logits
        gl = (jnp.where(counted, sigmoid(logits), 0.0) - event).astype(BF16)
        glog[:, rows] = gl
        gp = (tn(gl, w_hz[...]) * (q * (1.0 + pre * (1.0 - q)))).astype(BF16)
        gp2[rows, :] = gp
        ga = nt(gp, w_ns[...]).astype(BF16)
        for j in range(CHUNK):
            b = c * CHUNK + j
            spread = nn(turned[b], ga[j * BLK : (j + 1) * BLK])
            for k in range(K):
                i = b * K + k
                chain[i] = spread[k * BLK : (k + 1) * BLK] + chain[tab[t_prev + i]]

    def returned(q, rows):
        return chain[tab[t_last + NB + q], rows]

    b_post(returned, 0, PARTS // 4)

    def put(half, base, value):
        pack[half, :, pl.ds(base, rows_of), :] = (value * scale).reshape(groups, rows_of, D)

    put(0, rows_of, tn(agg2[...], gp2[...]))
    put(1, rows_of, tn(table2[pl.ds(0, NB)].reshape(NB * BLK, D), gp2[...]))
    hz = nn(glog[...], hid2[...]) * scale
    for t in range(TB // 8):
        pack[t // 2, t % 2, pl.ds(2 * rows_of, 8), :] = hz[t * 8 : (t + 1) * 8]
    loss = jnp.sum(loss_acc[...], keepdims=True) * scale
    pack[0, 2, pl.ds(2 * rows_of, 8), :] = jnp.broadcast_to(loss, (8, D))

    @pl.loop(0, CHUNKS)
    def _(c):
        rows = pl.ds(pl.multiple_of(c * ROWS, ROWS), ROWS)
        local = jnp.concatenate(
            [chain[tab[t_last + c * CHUNK + j]] for j in range(CHUNK)], axis=0
        )
        grad = local + nt(gp2[rows, :], w_ss[...]) + aux[rows, :].astype(F32)
        o_hidden[rows, :] = grad.astype(BF16)
        gp1[rows, :] = (grad * slope(pre1[rows, :])).astype(BF16)

    keeps[1].start()
    put(0, 0, tn(agg1[...], gp1[...]))
    put(1, 0, tn(own[...].reshape(NB * BLK, D), gp1[...]))

    swap = pltpu.make_async_remote_copy(
        src_ref=pack.at[1 - core], dst_ref=from_core, send_sem=core_sem.at[0],
        recv_sem=core_sem.at[1], device_id={"clus": sibling}, device_id_type=MESH,
    )
    swap.start()

    swap.wait()
    acc[...] = pack[core] + from_core[...]
    narrow[...] = acc[...].astype(BF16)

    def spread_out(p):
        return pltpu.make_async_remote_copy(
            src_ref=narrow.at[p], dst_ref=from_grp.at[g], send_sem=g_send.at[p],
            recv_sem=g_recv.at[g], device_id={"grp": p}, device_id_type=MESH,
        )

    for p in peers:
        spread_out(p).start()

    b_post(returned, PARTS // 4, 3)

    mine[...] = acc[g]

    @pl.loop(1, groups)
    def _(d):
        p = grp_peer(d)
        pltpu.make_async_remote_copy(
            src_ref=narrow.at[p], dst_ref=from_grp.at[p], send_sem=g_send.at[p],
            recv_sem=g_recv.at[p], device_id={"grp": p}, device_id_type=MESH,
        ).wait_recv()
        mine[...] += from_grp[p].astype(F32)

    def owner(u):
        return (u * depth) // units

    def lot(u):
        return u if depth < units else 0

    def unit_of(ref, u):
        return ref.at[pl.ds(8 * (u // 2), 8), pl.ds(LANES * (u % 2), LANES)]

    def to_owner(u):
        return pltpu.make_async_remote_copy(
            src_ref=unit_of(mine, u), dst_ref=from_z.at[lot(u), z], send_sem=z_send.at[u],
            recv_sem=z_recv.at[lot(u), z], device_id={"clus": owner(u) * 2 + core},
            device_id_type=MESH,
        )

    for u in range(units):
        @pl.when(z != owner(u))
        def _():
            to_owner(u).start()

    def share(u, d):
        q = z_peer(d)
        return pltpu.make_async_remote_copy(
            src_ref=unit_of(done, u), dst_ref=unit_of(done, u), send_sem=zb_send.at[lot(u), q],
            recv_sem=zb_recv.at[u], device_id={"clus": q * 2 + core}, device_id_type=MESH,
        )

    for u in range(units):
        @pl.when(z == owner(u))
        def _():
            def gather(d, partial):
                q = z_peer(d)
                pltpu.make_async_remote_copy(
                    src_ref=unit_of(mine, u), dst_ref=from_z.at[lot(u), q],
                    send_sem=z_send.at[u], recv_sem=z_recv.at[lot(u), q],
                    device_id={"clus": q * 2 + core}, device_id_type=MESH,
                ).wait_recv()
                return partial + from_z[lot(u), q]

            unit_of(done, u)[...] = lax.fori_loop(1, depth, gather, unit_of(mine, u)[...])

            @pl.loop(1, depth)
            def _(d):
                share(u, d).start()

    for u in range(units):
        @pl.when(z != owner(u))
        def _():
            to_owner(u).wait_send()
            share(u, 1).wait_recv()

    def publish(p, slot):
        return pltpu.make_async_remote_copy(
            src_ref=final, dst_ref=total.at[core, slot], send_sem=r_send.at[p],
            recv_sem=r_recv.at[slot], device_id={"grp": p}, device_id_type=MESH,
        )

    def forward(half, p):
        return pltpu.make_async_remote_copy(
            src_ref=total.at[half, p], dst_ref=total.at[half, p], send_sem=w_send.at[p],
            recv_sem=w_recv.at[p], device_id={"clus": sibling}, device_id_type=MESH,
        )

    final[...] = done[...].astype(BF16)

    for p in peers:
        publish(p, g).start()

    b_post(returned, 3, PARTS)
    total[core, g] = final[...]
    forward(core, g).start()

    @pl.loop(1, groups)
    def _(d):
        b_whole(grp_peer(d)).wait_recv()

    @pl.loop(0, slots)
    def _(i):
        fold[i] = came[i].astype(F32) + fold[tab[t_qprev + i]]

    @pl.loop(0, NB)
    def _(j):
        o_aux[pl.ds(j * BLK, BLK), :] = fold[tab[t_qlast + j]].astype(BF16)

    keeps[2].start()

    @pl.loop(1, groups)
    def _(d):
        p = grp_peer(d)
        publish(p, p).wait_recv()
        forward(core, p).start()

    @pl.loop(0, groups)
    def _(p):
        forward(1 - core, p).wait_recv()

    keeps[3].start()

    @pl.loop(1, groups)
    def _(d):
        h_whole(grp_peer(d)).wait_send()
        b_whole(grp_peer(d)).wait_send()
        spread_out(grp_peer(d)).wait_send()
        publish(grp_peer(d), g).wait_send()

    @pl.loop(0, groups)
    def _(p):
        forward(core, p).wait_send()

    for u in range(units):
        @pl.when(z == owner(u))
        def _():
            @pl.loop(1, depth)
            def _(d):
                share(u, d).wait_send()

    for keep in keeps:
        keep.wait()


def tail_kernel(groups, x_hist, x_hidden, x_aux, x_total,
                o_hist, o_hidden, o_aux, o_nf, o_sf, o_ns, o_ss, o_hz, o_loss,
                v_hist, v_hidden, v_aux, total, grads, into, out):
    rows_of = D // groups
    first = [
        pltpu.make_async_copy(a, b, into.at[i])
        for i, (a, b) in enumerate(
            ((x_total, total), (x_hist, v_hist), (x_hidden, v_hidden), (x_aux, v_aux))
        )
    ]
    second = [
        pltpu.make_async_copy(a, b, out.at[i])
        for i, (a, b) in enumerate(
            ((v_hist, o_hist), (v_hidden, o_hidden), (v_aux, o_aux), (grads.at[0], o_nf),
             (grads.at[1], o_sf), (grads.at[2], o_ns), (grads.at[3], o_ss))
        )
    ]
    for copy in first:
        copy.start()
    for t in range(1, 4):
        first[t].wait()
        second[t - 1].start()
    first[0].wait()
    for t, (half, base) in enumerate(((0, 0), (1, 0), (0, rows_of), (1, rows_of))):
        grads[t] = total[half, :, pl.ds(base, rows_of), :].astype(F32).reshape(D, D)
        second[3 + t].start()
    for t in range(TB // 8):
        o_hz[pl.ds(t * 8, 8), :] = total[t // 2, t % 2, pl.ds(2 * rows_of, 8), :].astype(F32)
    o_loss[...] = total[0, 2, pl.ds(2 * rows_of, 8), pl.ds(0, LANES)].astype(F32)[0:1, 0:1]
    for copy in second:
        copy.wait()


def latest(hit):
    count = hit.shape[1]
    place = lax.broadcasted_iota(jnp.int32, hit.shape, 1)
    found = jnp.max(jnp.where(hit, place, -1), axis=1)
    return jnp.where(found < 0, count, found)


def before(keys):
    shape = (keys.shape[0], keys.shape[0])
    earlier = lax.broadcasted_iota(jnp.int32, shape, 1) < lax.broadcasted_iota(jnp.int32, shape, 0)
    return latest((keys[None, :] == keys[:, None]) & earlier)


def holder(keys, count):
    return latest(keys[None, :] == lax.broadcasted_iota(jnp.int32, (count, keys.shape[0]), 0))


def shards(
    features, history, aux_history, tile_values, tile_sources, send_list, event_bins, event_flags,
    neigh_first, self_first, neigh_second, self_second, hazard_weight,
):
    groups = lax.axis_size("grp")
    depth = lax.axis_size("clus") // 2
    slots = groups * S
    rows_of = D // groups
    piece = 2 * rows_of + 8
    units = piece // 4
    lots = units if depth < units else 1
    src = tile_sources.reshape(TILES)
    snd = send_list.reshape(slots)
    tab = jnp.concatenate(
        [
            src, jnp.minimum(snd, NB - 1), before(src), holder(src, NB + slots), before(snd),
            holder(snd, NB),
        ]
    )
    any_spec = pl.BlockSpec(memory_space=pl.ANY)
    vmem = pl.BlockSpec(memory_space=pltpu.VMEM)
    dma = pltpu.SemaphoreType.DMA
    nodes = NB * BLK
    nodes_out = jax.ShapeDtypeStruct((nodes, D), BF16)
    weight_out = jax.ShapeDtypeStruct((D, D), F32)
    total_out = jax.ShapeDtypeStruct((2, groups, piece, D), BF16)
    scratch = [
        pltpu.VMEM((nodes, D), BF16),
        pltpu.VMEM((nodes, D), BF16),
        pltpu.VMEM((nodes, D), BF16),
        pltpu.VMEM((CHUNKS, 1, ROWS), jnp.int32),
        pltpu.VMEM((CHUNKS, 1, ROWS), jnp.int32),
        pltpu.VMEM((D, D), BF16),
        pltpu.VMEM((D, D), BF16),
        pltpu.VMEM((D, D), BF16),
        pltpu.VMEM((D, D), BF16),
        pltpu.VMEM((TB, D), BF16),
        pltpu.VMEM((NB, BLK, D), BF16),
        pltpu.VMEM((NB, BLK, D), BF16),
        pltpu.VMEM((nodes, D), BF16),
        pltpu.VMEM((NB, K, BLK, BLK), BF16),
        pltpu.VMEM((NB, K * BLK, BLK), BF16),
        pltpu.VMEM((NB + slots, BLK, D), BF16),
        pltpu.VMEM((NB + slots, BLK, D), BF16),
        pltpu.VMEM((slots, BLK, D), BF16),
        pltpu.VMEM((slots, BLK, D), BF16),
        pltpu.VMEM((nodes, D), BF16),
        pltpu.VMEM((nodes, D), BF16),
        pltpu.VMEM((nodes, D), F32),
        pltpu.VMEM((nodes, D), BF16),
        pltpu.VMEM((nodes, D), BF16),
        pltpu.VMEM((nodes, D), BF16),
        pltpu.VMEM((TB, nodes), BF16),
        pltpu.VMEM((TILES + 1, BLK, D), F32),
        pltpu.VMEM((slots, BLK, D), BF16),
        pltpu.VMEM((slots + 1, BLK, D), F32),
        pltpu.VMEM((TB, ROWS), F32),
        pltpu.VMEM((2, groups, piece, D), F32),
        pltpu.VMEM((2, groups, piece, D), BF16),
        pltpu.VMEM((groups, piece, D), F32),
        pltpu.VMEM((groups, piece, D), BF16),
        pltpu.VMEM((groups, piece, D), F32),
        pltpu.VMEM((groups, piece, D), BF16),
        pltpu.VMEM((piece, D), F32),
        pltpu.VMEM((lots, depth, 8, LANES), F32),
        pltpu.VMEM((piece, D), F32),
        pltpu.VMEM((piece, D), BF16),
        dma((12,)),
        dma((groups,)), dma((groups,)), dma((groups,)), dma((groups,)), dma((groups,)),
        dma((groups,)),
        dma((2,)), dma((groups,)), dma((groups,)), dma((units,)), dma((lots, depth)),
        dma((lots, depth)), dma((units,)), dma((groups,)), dma((groups,)), dma((groups,)),
        dma((groups,)),
    ]
    outs = pl.pallas_call(
        functools.partial(program_kernel, groups, depth),
        out_shape=(nodes_out,) * 3 + (total_out,),
        in_specs=[pl.BlockSpec(memory_space=pltpu.SMEM)] + [any_spec] * 11,
        out_specs=(any_spec,) * 4,
        scratch_shapes=scratch,
        compiler_params=pltpu.CompilerParams(
            collective_id=0, has_side_effects=True, vmem_limit_bytes=56 << 20
        ),
    )(
        tab,
        features.reshape(NB, BLK, D),
        history.reshape(NB, BLK, D),
        aux_history.reshape(nodes, D),
        tile_values.reshape(NB, K, BLK, BLK),
        event_bins.reshape(CHUNKS, 1, ROWS),
        event_flags.reshape(CHUNKS, 1, ROWS),
        neigh_first, self_first, neigh_second, self_second, hazard_weight.T,
    )
    hist, hidden, aux, nf, sf, ns, ss, hz, loss = pl.pallas_call(
        functools.partial(tail_kernel, groups),
        out_shape=(nodes_out,) * 3 + (weight_out,) * 4 + (
            jax.ShapeDtypeStruct((TB, D), F32), jax.ShapeDtypeStruct((1, 1), F32),
        ),
        in_specs=[any_spec] * 4,
        out_specs=(any_spec,) * 7 + (vmem,) * 2,
        scratch_shapes=[
            pltpu.VMEM((nodes, D), BF16),
            pltpu.VMEM((nodes, D), BF16),
            pltpu.VMEM((nodes, D), BF16),
            pltpu.VMEM((2, groups, piece, D), BF16),
            pltpu.VMEM((4, D, D), F32),
            dma((4,)),
            dma((7,)),
        ],
        compiler_params=pltpu.CompilerParams(vmem_limit_bytes=58 << 20),
    )(*outs)
    return (
        hist[None, None], hidden[None, None], aux[None, None],
        nf, sf, ns, ss, hz.T, loss[0, 0],
    )


def solution(mesh):
    in_specs = (
        P("clus", "grp", None, None),
        P("clus", "grp", None, None),
        P("clus", "grp", None, None),
        P("clus", "grp", None, None, None, None),
        P("clus", "grp", None, None),
        P("clus", "grp", None, None),
        P("clus", "grp", None),
        P("clus", "grp", None),
        P(), P(), P(), P(), P(),
    )
    out_specs = (
        P("clus", "grp", None, None),
        P("clus", "grp", None, None),
        P("clus", "grp", None, None),
        P(), P(), P(), P(), P(), P(),
    )
    return jax.shard_map(shards, mesh=mesh, in_specs=in_specs, out_specs=out_specs, check_vma=False)
```
